256 devices in a mesh: seq: 32 (over x, y, core), mp: 8 (over z).
Axes of the slice: x: 4, y: 4, z: 8, core: 2. Of those that a mesh axis runs over, the one named last changes fastest.
Arguments:
- hidden: bfloat16 [16, 4, 3584], P(None, None, 'seq'), may hold values from -40 to 40
- token_index_list: int32 [16, 4], replicated, may hold values from 0 to 31999
- embedding: bfloat16 [32000, 3584], P('mp', 'seq'), may hold values from -6 to 6
- attention_gain: bfloat16 [2, 3584], P(None, 'seq'), may hold values from 0.25 to 1.75
- query_key_value_matrix: bfloat16 [2, 3584, 3, 7168], P(None, 'seq', None, 'mp'), may hold values from -0.0625 to 0.0625
- attention_adapter_down: bfloat16 [2, 3584, 128], P(None, 'seq'), may hold values from -0.0625 to 0.0625
- attention_adapter_up: bfloat16 [128, 3, 7168], P(None, None, 'mp'), may hold values from -0.5 to 0.5
- cached_key_rows: bfloat16 [16, 4096, 7168], P(None, 'seq', 'mp'), may hold values from -240 to 240
- cached_value_rows: bfloat16 [16, 4096, 7168], P(None, 'seq', 'mp'), may hold values from -6 to 6
- lengths: int32 [16], replicated, may hold values from 1 to 4096, as said below
- output_matrix: bfloat16 [7168, 3584], P('mp', 'seq'), may hold values from -0.375 to 0.375
- feedforward_gain: bfloat16 [3584], P('seq'), may hold values from 0.25 to 1.75
- gate_matrix: bfloat16 [3584, 14336], P('seq', 'mp'), may hold values from -0.09375 to 0.09375
- up_matrix: bfloat16 [3584, 14336], P('seq', 'mp'), may hold values from -0.09375 to 0.09375
- feedforward_adapter_down: bfloat16 [3584, 128], P('seq'), may hold values from -0.09375 to 0.09375
- feedforward_adapter_up: bfloat16 [128, 2, 14336], P(None, None, 'mp'), may hold values from -0.5 to 0.5
- down_matrix: bfloat16 [14336, 3584], P('mp', 'seq'), may hold values from -0.046875 to 0.046875
Outputs:
- updated: bfloat16 [16, 4, 3584], P(None, None, 'seq')
- new_keys: bfloat16 [16, 4, 7168], P(None, None, 'mp')
- new_values: bfloat16 [16, 4, 7168], P(None, None, 'mp')
The draws below stay inside these ranges and needn't reach their ends.
Inputs may be any that keep to these rules, and one draw needn't show every extreme that they name: `lengths`: heavy tailed, even in the logarithm; one request's cache is full, of 4096 positions.
All inputs are finite; a program needn't handle non-finite values.
Results may differ from the reference program's by a relative error of at most 0.02.
The reference program's roundings to bfloat16 on the way count: a program that leaves them out, or rounds other values in their place, can miss the bound.
Values may be sent and summed in bfloat16 or wider, within the bound.
A program may use at most 128 MiB of HBM per device.

```python
import math
import jax
import jax.numpy as jnp
from jax import lax

MODEL_WIDTH = 3584
HEADS = 32
HEAD_DIM = 224
MLP_UNITS = 14336
ADAPTER_RANK = 128
VOCAB = 32000
NEW = 4
REQ = 16
ATTENTION_WIDTH = 7168
MAXLEN = 4096


def draw_hidden(key, part):
    k_base, k_rows, k_rough = jax.random.split(key, 3)
    rise = jnp.exp(jnp.arange(MODEL_WIDTH, dtype=jnp.float32) * (math.log(3.0) / MODEL_WIDTH))
    rough = jnp.exp(jax.random.uniform(k_rough, (MODEL_WIDTH,), jnp.float32, -0.7, 0.7))
    base = jnp.clip(jax.random.normal(k_base, (REQ, NEW, MODEL_WIDTH), jnp.float32), -6.0, 6.0)
    scales = jnp.exp(jax.random.uniform(k_rows, (REQ, NEW, 1), jnp.float32, math.log(0.03), math.log(0.4)))
    return (base * scales * rise * rough).astype(jnp.bfloat16)


def draw_cached_key_rows(key, part):
    k_base = jax.random.fold_in(key, 0)
    base = jnp.clip(jax.random.normal(k_base, (REQ, MAXLEN, ATTENTION_WIDTH), jnp.float32), -6.0, 6.0)
    return base.astype(jnp.bfloat16)


def draw_lengths(key, part):
    k_power, k_extra, k_chosen = jax.random.split(key, 3)
    power = jax.random.randint(k_power, (REQ,), 4, 13)
    ceiling = jnp.minimum(jnp.left_shift(jnp.int32(1), power), MAXLEN)
    floor_len = ceiling // 2
    extra = jax.random.randint(k_extra, (REQ,), 0, 1 << 20) % (ceiling - floor_len)
    length = floor_len + 1 + extra
    chosen = jax.random.randint(k_chosen, (), 0, REQ)
    return jnp.where(jnp.arange(REQ) == chosen, MAXLEN, length).astype(jnp.int32)


def touch_ends(array, key, low, high):
    extent = array.shape
    place = [jax.random.randint(jax.random.fold_in(key, axis), (), 0, extent[axis]) for axis in range(len(extent))]
    array = array.at[tuple(place)].set(low)
    longest = extent.index(max(extent))
    place[longest] = (place[longest] + 1) % extent[longest]
    return array.at[tuple(place)].set(high)


def shard_levels(key, extent, shards, least, largest):
    def one(dim, shards_of):
        draws = jax.random.uniform(jax.random.fold_in(jax.random.fold_in(key, 6), dim), (shards_of,), jnp.float32, least / len(shards), largest / len(shards))
        return jnp.repeat(jnp.exp(draws), extent[dim] // shards_of).reshape((-1,) + (1,) * (len(extent) - dim - 1))

    factor_of = one(*shards[0])
    for cut in shards[1:]:
        factor_of = factor_of * one(*cut)
    return factor_of


def gaussian(own_key, dims, spread, limit, shards=(), held_as=jnp.bfloat16):
    drawn = jax.random.normal(own_key, dims, jnp.float32) * spread
    if len(shards) > 0:
        drawn = shard_levels(own_key, dims, shards, -0.22, 0.18) * drawn
    return jnp.clip(drawn, min=-limit, max=limit).astype(held_as)


def setup_inputs(seed: int = 0) -> dict:
    key_of = jax.random.split(jax.random.key(seed), 18)
    hidden = draw_hidden(jax.random.fold_in(key_of[17], 71), 0)
    token_index_list = touch_ends(jax.random.randint(key_of[1], (REQ, NEW), 0, VOCAB), jax.random.fold_in(key_of[1], 1), 0, VOCAB - 1).astype(jnp.int32)
    embedding = gaussian(key_of[2], (VOCAB, MODEL_WIDTH), 1.0, 6.0, ((0, 8), (1, 32)))
    attention_gain = jnp.clip(1.0 + 0.15 * jax.random.normal(key_of[3], (2, MODEL_WIDTH), jnp.float32), 0.25, 1.75).astype(jnp.bfloat16)
    query_key_value_matrix = gaussian(key_of[4], (2, MODEL_WIDTH, 3, ATTENTION_WIDTH), (2 * MODEL_WIDTH) ** -0.5, 0.0625, ((1, 32), (3, 8)))
    attention_adapter_down = gaussian(key_of[5], (2, MODEL_WIDTH, ADAPTER_RANK), (2 * MODEL_WIDTH) ** -0.5, 0.0625, ((1, 32),))
    attention_adapter_up = gaussian(key_of[6], (ADAPTER_RANK, 3, ATTENTION_WIDTH), ADAPTER_RANK ** -0.5, 0.5, ((2, 8),))
    cached_key_rows = draw_cached_key_rows(jax.random.fold_in(key_of[17], 71), 0)
    cached_value_rows = gaussian(key_of[8], (REQ, MAXLEN, ATTENTION_WIDTH), 1.0, 6.0, ((1, 32), (2, 8)))
    lengths = draw_lengths(jax.random.fold_in(key_of[17], 71), 0)
    output_matrix = gaussian(key_of[10], (ATTENTION_WIDTH, MODEL_WIDTH), HEAD_DIM ** -0.5, 0.375, ((0, 8), (1, 32)))
    feedforward_gain = jnp.clip(1.0 + 0.15 * jax.random.normal(key_of[11], (MODEL_WIDTH,), jnp.float32), 0.25, 1.75).astype(jnp.bfloat16)
    gate_matrix = gaussian(key_of[12], (MODEL_WIDTH, MLP_UNITS), MODEL_WIDTH ** -0.5, 0.09375, ((0, 32), (1, 8)))
    up_matrix = gaussian(key_of[13], (MODEL_WIDTH, MLP_UNITS), MODEL_WIDTH ** -0.5, 0.09375, ((0, 32), (1, 8)))
    feedforward_adapter_down = gaussian(key_of[14], (MODEL_WIDTH, ADAPTER_RANK), MODEL_WIDTH ** -0.5, 0.09375, ((0, 32),))
    feedforward_adapter_up = gaussian(key_of[15], (ADAPTER_RANK, 2, MLP_UNITS), ADAPTER_RANK ** -0.5, 0.5, ((2, 8),))
    down_matrix = gaussian(key_of[16], (MLP_UNITS, MODEL_WIDTH), MLP_UNITS ** -0.5, 0.046875, ((0, 8), (1, 32)))
    return dict(hidden=hidden, token_index_list=token_index_list, embedding=embedding, attention_gain=attention_gain, query_key_value_matrix=query_key_value_matrix, attention_adapter_down=attention_adapter_down, attention_adapter_up=attention_adapter_up, cached_key_rows=cached_key_rows, cached_value_rows=cached_value_rows, lengths=lengths, output_matrix=output_matrix, feedforward_gain=feedforward_gain, gate_matrix=gate_matrix, up_matrix=up_matrix, feedforward_adapter_down=feedforward_adapter_down, feedforward_adapter_up=feedforward_adapter_up, down_matrix=down_matrix)


epsilon = 1e-05
masked_score = -1e+30

def reference(hidden, token_index_list, embedding, attention_gain, query_key_value_matrix, attention_adapter_down, attention_adapter_up, cached_key_rows, cached_value_rows, lengths, output_matrix, feedforward_gain, gate_matrix, up_matrix, feedforward_adapter_down, feedforward_adapter_up, down_matrix):
    row_count = REQ * NEW
    flat_ids = token_index_list.reshape(row_count).astype(jnp.int32)
    embedded = jnp.take(embedding, flat_ids, axis=0)
    state_f = hidden.reshape(row_count, MODEL_WIDTH).astype(jnp.float32)
    embed_f = embedded.astype(jnp.float32)
    squares = lax.optimization_barrier(jnp.sum(state_f * state_f, 1)) + lax.optimization_barrier(jnp.sum(embed_f * embed_f, 1))
    attention_scale = 1.0 / jnp.sqrt(squares / (2 * MODEL_WIDTH) + epsilon)
    gains = attention_gain.astype(jnp.float32)
    scaled_hidden = (state_f * gains[0]).astype(jnp.bfloat16)
    scaled_embedding = (embed_f * gains[1]).astype(jnp.bfloat16)
    wide_h = query_key_value_matrix[0].reshape(MODEL_WIDTH, 3 * ATTENTION_WIDTH)
    wide_e = query_key_value_matrix[1].reshape(MODEL_WIDTH, 3 * ATTENTION_WIDTH)
    adapter_total = jnp.dot(scaled_hidden, attention_adapter_down[0], preferred_element_type=jnp.float32) + jnp.dot(scaled_embedding, attention_adapter_down[1], preferred_element_type=jnp.float32)
    attention_adapter_state = (adapter_total * attention_scale[:, None]).astype(jnp.bfloat16)
    projection_total = jnp.dot(scaled_hidden, wide_h, preferred_element_type=jnp.float32) + jnp.dot(scaled_embedding, wide_e, preferred_element_type=jnp.float32)
    projected_rows = projection_total * attention_scale[:, None] + jnp.dot(attention_adapter_state, attention_adapter_up.reshape(ADAPTER_RANK, 3 * ATTENTION_WIDTH), preferred_element_type=jnp.float32)
    projected_rows = projected_rows.astype(jnp.bfloat16).reshape(REQ, NEW, 3, HEADS, HEAD_DIM)
    queries = projected_rows[:, :, 0]
    fresh_keys = projected_rows[:, :, 1]
    fresh_values = projected_rows[:, :, 2]
    inv_scale = 1.0 / jnp.sqrt(jnp.float32(HEAD_DIM))
    causal = jnp.arange(NEW)[:, None] >= jnp.arange(NEW)[None, :]
    positions = jnp.arange(MAXLEN, dtype=jnp.int32)

    def one_request(items):
        query_b, key_new, value_new, keys_b, values_b, length_b = items
        keys_b = keys_b.reshape(MAXLEN, HEADS, HEAD_DIM).astype(jnp.float32)
        values_b = values_b.reshape(MAXLEN, HEADS, HEAD_DIM).astype(jnp.float32)
        query_f = query_b.astype(jnp.float32)
        live_mask = positions < length_b
        cache_scores = jnp.einsum('thd,phd->htp', query_f, keys_b) * inv_scale
        cache_scores = jnp.where(live_mask[None, None, :], cache_scores, masked_score)
        new_scores = jnp.einsum('thd,jhd->htj', query_f, key_new.astype(jnp.float32)) * inv_scale
        new_scores = jnp.where(causal[None], new_scores, masked_score)
        peak = jnp.maximum(lax.optimization_barrier(jnp.max(cache_scores, -1)), lax.optimization_barrier(jnp.max(new_scores, -1)))
        cache_w = jnp.where(live_mask[None, None, :], jnp.exp(cache_scores - peak[..., None]), 0.0)
        new_w = jnp.where(causal[None], jnp.exp(new_scores - peak[..., None]), 0.0)
        row_total = lax.optimization_barrier(jnp.sum(cache_w, -1)) + lax.optimization_barrier(jnp.sum(new_w, -1))
        cache_wb = lax.optimization_barrier(cache_w.astype(jnp.bfloat16)).astype(jnp.float32)
        new_wb = lax.optimization_barrier(new_w.astype(jnp.bfloat16)).astype(jnp.float32)
        numer = jnp.einsum('htp,phd->thd', cache_wb, values_b) + jnp.einsum('htj,jhd->thd', new_wb, value_new.astype(jnp.float32))
        return numer / jnp.transpose(row_total)[:, :, None]
    attended = lax.map(one_request, (queries, fresh_keys, fresh_values, cached_key_rows, cached_value_rows, lengths))
    attended = attended.reshape(row_count, ATTENTION_WIDTH).astype(jnp.bfloat16)
    mid = state_f + jnp.dot(attended, output_matrix, preferred_element_type=jnp.float32)
    feedforward_scale = 1.0 / jnp.sqrt(lax.optimization_barrier(jnp.sum(mid * mid, 1)) / MODEL_WIDTH + epsilon)
    scaled_feedforward = (mid * feedforward_gain.astype(jnp.float32)).astype(jnp.bfloat16)
    feedforward_adapter_state = (jnp.dot(scaled_feedforward, feedforward_adapter_down, preferred_element_type=jnp.float32) * feedforward_scale[:, None]).astype(jnp.bfloat16)
    gate_values = jnp.dot(scaled_feedforward, gate_matrix, preferred_element_type=jnp.float32) * feedforward_scale[:, None] + jnp.dot(feedforward_adapter_state, feedforward_adapter_up[:, 0], preferred_element_type=jnp.float32)
    up_piece = jnp.dot(scaled_feedforward, up_matrix, preferred_element_type=jnp.float32) * feedforward_scale[:, None] + jnp.dot(feedforward_adapter_state, feedforward_adapter_up[:, 1], preferred_element_type=jnp.float32)
    activated = (jax.nn.gelu(gate_values, approximate=True) * up_piece).astype(jnp.bfloat16)
    updated = (mid + jnp.dot(activated, down_matrix, preferred_element_type=jnp.float32)).astype(jnp.bfloat16)
    return (updated.reshape(REQ, NEW, MODEL_WIDTH), fresh_keys.reshape(REQ, NEW, ATTENTION_WIDTH), fresh_values.reshape(REQ, NEW, ATTENTION_WIDTH))
```

```python
import jax
import jax.numpy as jnp
from jax import lax
from jax.experimental import pallas as pl
from jax.experimental.pallas import tpu as pltpu
from jax.sharding import PartitionSpec as P

MODEL_WIDTH = 3584
HEAD_DIM = 224
EPS = 1e-05
DEAD = -1e30

NS = 32
NM = 8
ROWS = 64
F = 112
FP = 128
CW = 896
HEADS = 4
UW = 1792
POS = 128
VR = 4000
REQ = 16
TOK = 4
RT = 16
NI = ROWS // RT
NJ = 7
OWN = NI * NJ

BF = jnp.bfloat16
F32 = jnp.float32
MESH = pl.DeviceIdType.MESH

DIMS_NT = (((1,), (1,)), ((), ()))


def mm(a, b):
    return jnp.dot(a, b, preferred_element_type=F32)


def mm_nt(a, b):
    return lax.dot_general(a, b, DIMS_NT, preferred_element_type=F32)


def head_of(col):
    one = jnp.int32(1)
    zero = jnp.int32(0)
    return (
        jnp.where(col >= HEAD_DIM, one, zero)
        + jnp.where(col >= 2 * HEAD_DIM, one, zero)
        + jnp.where(col >= 3 * HEAD_DIM, one, zero)
    )


def kernel(
    ids_hbm,
    len_hbm,
    hid_hbm,
    emb_hbm,
    gain_hbm,
    wqkv_hbm,
    adown_hbm,
    aup_hbm,
    kc_hbm,
    vc_hbm,
    wout_hbm,
    fgain_hbm,
    gate_hbm,
    upm_hbm,
    fdown_hbm,
    fup_hbm,
    down_hbm,
    upd_out,
    key_out,
    val_out,
    ids_v,
    len_s,
    hid_v,
    emb_v,
    gain_v,
    wq_v,
    ad_v,
    aup_v,
    kc_v,
    vc_v,
    wo_v,
    fgain_v,
    gate_v,
    upm_v,
    fd_v,
    fup_v,
    fu_v,
    dn_v,
    h_v,
    es_v,
    s2_v,
    r2_v,
    g_v,
    qm_v,
    s4_v,
    r4_v,
    a_v,
    hp_v,
    hr_v,
    mid_v,
    s7_v,
    r7_v,
    a2_v,
    dp_v,
    dr_v,
    fin_v,
    upd_v,
    key_v,
    val_v,
    lsem,
    ssem,
    rsem,
):
    me_s = lax.axis_index("seq")
    me_m = lax.axis_index("mp")
    mine = me_s < OWN
    my_i = lax.div(me_s, NJ)
    my_j = lax.rem(me_s, NJ)
    my_i = jnp.where(mine, my_i, 0)
    my_j = jnp.where(mine, my_j, 0)
    my_rows = pl.ds(pl.multiple_of(my_i * RT, RT), RT)

    barrier = pltpu.get_barrier_semaphore()

    def loop(n, me, fn):
        def body(k, carry):
            fn(lax.rem(me + 1 + k, n))
            return carry

        lax.fori_loop(0, n - 1, body, 0)

    def greet(axis):
        def fn(p):
            pl.semaphore_signal(barrier, inc=1, device_id={axis: p}, device_id_type=MESH)

        return fn

    loop(NS, me_s, greet("seq"))
    loop(NM, me_m, greet("mp"))

    local = []

    def fetch(src, dst):
        copy = pltpu.make_async_copy(src, dst, lsem.at[len(local)])
        copy.start()
        local.append(copy)
        return copy

    c_ids = fetch(ids_hbm, ids_v)
    c_emb = fetch(emb_hbm, emb_v)
    c_hid = fetch(hid_hbm, hid_v)
    c_gain = fetch(gain_hbm, gain_v)
    c_ad0 = fetch(adown_hbm.at[0], ad_v.at[pl.ds(0, F)])
    c_ad1 = fetch(adown_hbm.at[1], ad_v.at[pl.ds(FP, F)])
    c_wq0 = fetch(wqkv_hbm.at[0], wq_v.at[:, pl.ds(0, F)])
    c_wq1 = fetch(wqkv_hbm.at[1], wq_v.at[:, pl.ds(FP, F)])
    c_aup = fetch(aup_hbm, aup_v)
    c_len = fetch(len_hbm, len_s)
    c_kc = fetch(kc_hbm, kc_v)
    c_vc = fetch(vc_hbm, vc_v)
    c_wo = fetch(wout_hbm, wo_v.at[pl.ds(0, F)])
    c_fg = fetch(fgain_hbm, fgain_v)
    c_fup = fetch(fup_hbm, fup_v)
    c_fd = fetch(fdown_hbm, fd_v.at[pl.ds(0, F)])
    c_gate = fetch(gate_hbm, gate_v.at[pl.ds(0, F)])
    c_upm = fetch(upm_hbm, upm_v.at[pl.ds(0, F)])
    c_dn = fetch(down_hbm, dn_v.at[pl.ds(0, F)])

    pad = FP - F
    wq_v[:, pl.ds(F, pad), :] = jnp.zeros((3, pad, CW), BF)
    wq_v[:, pl.ds(FP + F, pad), :] = jnp.zeros((3, pad, CW), BF)
    ad_v[pl.ds(F, pad), :] = jnp.zeros((pad, FP), BF)
    ad_v[pl.ds(FP + F, pad), :] = jnp.zeros((pad, FP), BF)
    wo_v[pl.ds(F, pad), :] = jnp.zeros((pad, CW), BF)
    fd_v[pl.ds(F, pad), :] = jnp.zeros((pad, FP), BF)
    gate_v[pl.ds(F, pad), :] = jnp.zeros((pad, UW), BF)
    upm_v[pl.ds(F, pad), :] = jnp.zeros((pad, UW), BF)
    dn_v[pl.ds(F, pad), :] = jnp.zeros((pad, UW), BF)
    h_v[...] = jnp.zeros((ROWS, FP), F32)

    def took(ref, sem):
        pltpu.make_async_copy(ref, ref, sem).wait()

    def send(src, dst, phase, axis, p):
        pltpu.make_async_remote_copy(
            src_ref=src,
            dst_ref=dst,
            send_sem=ssem.at[phase],
            recv_sem=rsem.at[phase],
            device_id={axis: p},
            device_id_type=MESH,
        ).start()

    def scatter(src_of, dst, phase):
        def fn(p):
            @pl.when(p < OWN)
            def _():
                send(src_of(lax.div(p, NJ), lax.rem(p, NJ)), dst, phase, "seq", p)

        loop(NS, me_s, fn)

    def gather(ref, phase):
        loop(NS, me_s, lambda p: send(ref, ref, phase, "seq", p))

    c_ids.wait()
    ids = ids_v[...]
    high = ids // 256
    low = ids - high * 256
    spread = (
        lax.broadcasted_iota(jnp.int32, (REQ, ROWS), 0)
        == lax.broadcasted_iota(jnp.int32, (REQ, ROWS), 1) // TOK
    ).astype(F32).astype(BF)
    wide = mm(high.astype(F32).astype(BF), spread) * 256.0 + mm(low.astype(F32).astype(BF), spread)
    pick = lax.broadcasted_iota(jnp.int32, (TOK, ROWS), 0) == (
        lax.broadcasted_iota(jnp.int32, (TOK, ROWS), 1) % TOK
    )
    id_row = jnp.sum(jnp.where(pick, wide, 0.0), 0, keepdims=True).astype(jnp.int32)
    id_row = id_row - me_m * VR
    selector = (
        (lax.broadcasted_iota(jnp.int32, (VR, ROWS), 0) == id_row).astype(F32).astype(BF)
    )
    c_emb.wait()
    found = mm(emb_v[...], selector)
    found = jnp.concatenate([found, jnp.zeros((pad, ROWS), F32)], 0)
    es_v[me_m] = found.T.astype(BF)

    pl.semaphore_wait(barrier, NS + NM - 2)

    loop(NM, me_m, lambda p: send(es_v.at[me_m], es_v.at[me_m], 0, "mp", p))

    c_hid.wait()
    c_gain.wait()
    for b in range(REQ):
        h_v[pl.ds(TOK * b, TOK), pl.ds(0, F)] = hid_v[b].astype(F32)
    gains = gain_v[...].astype(F32)
    gains = jnp.concatenate([gains, jnp.zeros((2, pad), F32)], 1)
    state = h_v[...]
    scaled_h = (state * gains[0:1]).astype(BF)
    c_ad0.wait()
    c_ad1.wait()
    c_wq0.wait()
    c_wq1.wait()
    c_aup.wait()

    took(es_v.at[pl.ds(0, NM - 1)], rsem.at[0])
    embed = es_v[0].astype(F32)
    for q in range(1, NM):
        embed = embed + es_v[q].astype(F32)
    scaled_e = (embed * gains[1:2]).astype(BF)
    both = jnp.concatenate([scaled_h, scaled_e], 1)
    squares = jnp.sum(state * state + embed * embed, 1, keepdims=True)
    squares = jnp.broadcast_to(squares, (ROWS, 128)).astype(BF)
    low1 = mm(both, ad_v[...]).astype(BF)
    for part in range(3):
        proj = mm(both, wq_v[part]) + mm(low1, aup_v[part])
        for j in range(NJ):
            s2_v[j, :, pl.ds(128 * part, 128)] = proj[:, 128 * j : 128 * j + 128].astype(BF)
    for j in range(NJ):
        s2_v[j, :, pl.ds(384, 128)] = squares

    def block2(i, j):
        return s2_v.at[j, pl.ds(pl.multiple_of(i * RT, RT), RT)]

    scatter(block2, r2_v.at[me_s], 1)

    @pl.when(mine)
    def _():
        r2_v[me_s] = s2_v[my_j, my_rows, :]
        took(r2_v.at[pl.ds(0, NS - 1)], rsem.at[1])
        total = r2_v[0].astype(F32)
        for s in range(1, NS):
            total = total + r2_v[s].astype(F32)
        scale = 1.0 / jnp.sqrt(total[:, 384:] / (2 * MODEL_WIDTH) + EPS)
        for part in range(3):
            g_v[my_j, my_rows, pl.ds(128 * part, 128)] = (
                total[:, 128 * part : 128 * part + 128] * scale
            ).astype(BF)
        gather(g_v.at[my_j, my_rows], 2)
        took(r2_v.at[pl.ds(0, OWN - 1), :, pl.ds(0, 384)], rsem.at[2])

    @pl.when(jnp.logical_not(mine))
    def _():
        took(r2_v.at[pl.ds(0, OWN), :, pl.ds(0, 384)], rsem.at[2])

    lane = lax.broadcasted_iota(jnp.int32, (RT, 128), 1)
    for i in range(NI):
        rows = pl.ds(RT * i, RT)
        for c in range(NJ):
            q = g_v[c, rows, pl.ds(0, 128)].astype(F32)
            first, last = (128 * c) // HEAD_DIM, (128 * c + 127) // HEAD_DIM
            for h in range(HEADS):
                if first == last == h:
                    part = q
                elif h in (first, last):
                    part = jnp.where(head_of(lane + 128 * c) == h, q, 0.0)
                else:
                    part = jnp.zeros((RT, 128), F32)
                qm_v[i, pl.ds(RT * h, RT), pl.ds(128 * c, 128)] = part.astype(BF)

    inv_scale = 1.0 / (HEAD_DIM**0.5)
    c_len.wait()
    c_kc.wait()
    c_vc.wait()
    place = me_s * POS + lax.broadcasted_iota(jnp.int32, (HEADS * RT, POS), 1)
    group = (lax.broadcasted_iota(jnp.int32, (HEADS * RT, POS), 0) % RT) // TOK
    for i in range(NI):
        score = jnp.full((HEADS * RT, POS), DEAD, F32)
        for k in range(RT // TOK):
            b = (RT // TOK) * i + k
            one = mm_nt(qm_v[i], kc_v[b]) * inv_scale
            score = jnp.where((group == k) & (place < len_s[b]), one, score)
        peak = jnp.max(score, 1, keepdims=True)
        weight = jnp.where(score > 0.5 * DEAD, jnp.exp(score - peak), 0.0)
        total = jnp.sum(weight, 1, keepdims=True)
        spread_w = jnp.concatenate(
            [jnp.where(group == k, weight, 0.0).astype(BF) for k in range(RT // TOK)], 1
        )
        values = vc_v[pl.ds((RT // TOK) * i, RT // TOK)].reshape((RT // TOK) * POS, CW)
        numer = mm(spread_w, values)
        live = total > 0.0
        safe = jnp.where(live, total, 1.0)
        lse = jnp.where(live, peak + jnp.log(safe), DEAD)
        inverse = 1.0 / safe
        stats = jnp.zeros((RT, 128), F32)
        for h in range(HEADS):
            rest = jnp.broadcast_to(lse[RT * h : RT * h + RT], (RT, 128))
            for piece in range(3):
                lead = rest.astype(BF).astype(F32)
                stats = jnp.where(lane == 3 * h + piece, lead, stats)
                rest = rest - lead
        stats = stats.astype(BF)
        rows = pl.ds(RT * i, RT)
        for c in range(NJ):
            first, last = (128 * c) // HEAD_DIM, (128 * c + 127) // HEAD_DIM
            cols = slice(128 * c, 128 * c + 128)
            here = numer[RT * first : RT * first + RT, cols] * inverse[RT * first : RT * first + RT]
            if last != first:
                there = numer[RT * last : RT * last + RT, cols] * inverse[RT * last : RT * last + RT]
                here = jnp.where(head_of(lane + 128 * c) == first, here, there)
            s4_v[c, rows, pl.ds(0, 128)] = here.astype(BF)
            s4_v[c, rows, pl.ds(128, 128)] = stats

    def block4(i, j):
        return s4_v.at[j, pl.ds(pl.multiple_of(i * RT, RT), RT)]

    scatter(block4, r4_v.at[me_s], 3)

    @pl.when(mine)
    def _():
        r4_v[me_s] = s4_v[my_j, my_rows, :]
        lane_head = head_of(lane + 128 * my_j)
        head_a = head_of(128 * my_j)
        head_b = head_of(128 * my_j + 127)
        q = jnp.concatenate([g_v[c, my_rows, pl.ds(0, 128)] for c in range(NJ)], 1).astype(F32)
        k = jnp.concatenate([g_v[c, my_rows, pl.ds(128, 128)] for c in range(NJ)], 1)
        v = g_v[my_j, my_rows, pl.ds(256, 128)]
        col_head = head_of(lax.broadcasted_iota(jnp.int32, (RT, CW), 1))
        r_at = lax.broadcasted_iota(jnp.int32, (RT, RT), 0)
        c_at = lax.broadcasted_iota(jnp.int32, (RT, RT), 1)
        seen = (r_at // TOK == c_at // TOK) & (c_at % TOK <= r_at % TOK)

        def fresh(head):
            score = mm_nt(jnp.where(col_head == head, q, 0.0).astype(BF), k) * inv_scale
            score = jnp.where(seen, score, DEAD)
            peak = jnp.max(score, 1, keepdims=True)
            weight = jnp.where(seen, jnp.exp(score - peak), 0.0)
            total = jnp.sum(weight, 1, keepdims=True)
            return mm(weight.astype(BF), v) / total, peak + jnp.log(total)

        out_a, lse_a = fresh(head_a)
        out_b, lse_b = fresh(head_b)
        new_out = jnp.where(lane_head == head_a, out_a, out_b)
        new_lse = jnp.where(lane_head == head_a, lse_a, lse_b)

        stat_head = lax.broadcasted_iota(jnp.int32, (128, 128), 0) // 3
        expand = (
            (stat_head == head_of(lax.broadcasted_iota(jnp.int32, (128, 128), 1) + 128 * my_j))
            .astype(F32)
            .astype(BF)
        )
        took(r4_v.at[pl.ds(0, NS - 1)], rsem.at[3])
        stats = r4_v[:, :, pl.ds(128, 128)].reshape(NS * RT, 128)
        lse = mm(stats, expand).reshape(NS, RT, 128)
        peak = jnp.maximum(jnp.max(lse, 0), new_lse)
        weight = jnp.exp(lse - peak[None])
        new_weight = jnp.exp(new_lse - peak)
        total = jnp.sum(weight, 0) + new_weight
        numer = jnp.sum(weight * r4_v[:, :, pl.ds(0, 128)].astype(F32), 0) + new_weight * new_out
        block = a_v.at[my_rows, pl.ds(pl.multiple_of(my_j * 128, 128), 128)]
        block[...] = (numer / total).astype(BF)
        gather(block, 4)

    for b in range(REQ):
        for c in range(NJ):
            key_v[b, :, pl.ds(128 * c, 128)] = g_v[c, pl.ds(TOK * b, TOK), pl.ds(128, 128)]
            val_v[b, :, pl.ds(128 * c, 128)] = g_v[c, pl.ds(TOK * b, TOK), pl.ds(256, 128)]
    o_key = pltpu.make_async_copy(key_v, key_out, lsem.at[len(local)])
    o_val = pltpu.make_async_copy(val_v, val_out, lsem.at[len(local) + 1])
    o_key.start()
    o_val.start()
    c_fup.wait()

    def split(k, carry):
        at = pl.ds(pl.multiple_of(k * 16, 16), 16)
        two = fup_v[at].astype(F32)
        fu_v[0, at, :] = two[:, 0, :].astype(BF)
        fu_v[1, at, :] = two[:, 1, :].astype(BF)
        return carry

    lax.fori_loop(0, 8, split, 0)
    c_wo.wait()

    @pl.when(mine)
    def _():
        took(r4_v.at[pl.ds(0, OWN - 1), :, pl.ds(0, 128)], rsem.at[4])

    @pl.when(jnp.logical_not(mine))
    def _():
        took(r4_v.at[pl.ds(0, OWN), :, pl.ds(0, 128)], rsem.at[4])

    my_eight = pl.ds(pl.multiple_of(me_m * 8, 8), 8)

    def sum_mp(part_v, slot_v, phase):
        def fn(p):
            send(
                part_v.at[pl.ds(pl.multiple_of(p * 8, 8), 8)], slot_v.at[me_m], phase, "mp", p
            )

        loop(NM, me_m, fn)
        slot_v[me_m] = part_v[my_eight, :]
        took(slot_v.at[pl.ds(0, NM - 1)], rsem.at[phase])
        total = slot_v[0]
        for q in range(1, NM):
            total = total + slot_v[q]
        return total

    hp_v[...] = mm_nt(a_v[...], wo_v[...])
    mixed = sum_mp(hp_v, hr_v, 5)
    mid_v[my_eight, :] = mixed + h_v[my_eight, :]
    loop(NM, me_m, lambda p: send(mid_v.at[my_eight], mid_v.at[my_eight], 6, "mp", p))
    c_fg.wait()
    c_fd.wait()
    c_gate.wait()
    c_upm.wait()
    fgain = jnp.concatenate([fgain_v[...].astype(F32), jnp.zeros((1, pad), F32)], 1)
    took(hr_v.at[pl.ds(0, NM - 1)], rsem.at[6])

    mid = mid_v[...]
    scaled_m = (mid * fgain).astype(BF)
    squares = jnp.broadcast_to(jnp.sum(mid * mid, 1, keepdims=True), (ROWS, 128)).astype(BF)
    low2 = mm(scaled_m, fd_v[...]).astype(BF)
    for part, w_v in enumerate((gate_v, upm_v)):
        proj = mm(scaled_m, w_v[...]) + mm(low2, fu_v[part])
        for j in range(NJ):
            s7_v[j, :, pl.ds(256 * part, 256)] = proj[:, 256 * j : 256 * j + 256].astype(BF)
    for j in range(NJ):
        s7_v[j, :, pl.ds(512, 128)] = squares

    def block7(i, j):
        return s7_v.at[j, pl.ds(pl.multiple_of(i * RT, RT), RT)]

    scatter(block7, r7_v.at[me_s], 7)

    @pl.when(mine)
    def _():
        r7_v[me_s] = s7_v[my_j, my_rows, :]
        took(r7_v.at[pl.ds(0, NS - 1)], rsem.at[7])
        total = r7_v[0].astype(F32)
        for s in range(1, NS):
            total = total + r7_v[s].astype(F32)
        scale = 1.0 / jnp.sqrt(total[:, 512:] / MODEL_WIDTH + EPS)
        scale = jnp.concatenate([scale, scale], 1)
        gate = total[:, 0:256] * scale
        up = total[:, 256:512] * scale
        block = a2_v.at[my_rows, pl.ds(pl.multiple_of(my_j * 256, 256), 256)]
        block[...] = (jax.nn.gelu(gate, approximate=True) * up).astype(BF)
        gather(block, 8)
        took(r4_v.at[pl.ds(0, OWN - 1)], rsem.at[8])

    @pl.when(jnp.logical_not(mine))
    def _():
        took(r4_v.at[pl.ds(0, OWN)], rsem.at[8])

    c_dn.wait()
    dp_v[...] = mm_nt(a2_v[...], dn_v[...])
    down = sum_mp(dp_v, dr_v, 9)
    fin_v[my_eight, :] = down + mid_v[my_eight, :]
    loop(NM, me_m, lambda p: send(fin_v.at[my_eight], fin_v.at[my_eight], 10, "mp", p))
    took(dr_v.at[pl.ds(0, NM - 1)], rsem.at[10])
    for b in range(REQ):
        upd_v[b] = fin_v[pl.ds(TOK * b, TOK), pl.ds(0, F)].astype(BF)
    o_upd = pltpu.make_async_copy(upd_v, upd_out, lsem.at[len(local) + 2])
    o_upd.start()

    took(es_v.at[pl.ds(0, NM - 1)], ssem.at[0])
    took(hr_v.at[pl.ds(0, NM - 1)], ssem.at[5])
    took(hr_v.at[pl.ds(0, NM - 1)], ssem.at[6])
    took(dr_v.at[pl.ds(0, NM - 1)], ssem.at[9])
    took(dr_v.at[pl.ds(0, NM - 1)], ssem.at[10])

    @pl.when(mine)
    def _():
        took(r2_v.at[pl.ds(0, OWN - 1)], ssem.at[1])
        took(r2_v.at[pl.ds(0, NS - 1), :, pl.ds(0, 384)], ssem.at[2])
        took(r4_v.at[pl.ds(0, OWN - 1)], ssem.at[3])
        took(r4_v.at[pl.ds(0, NS - 1), :, pl.ds(0, 128)], ssem.at[4])
        took(r7_v.at[pl.ds(0, OWN - 1)], ssem.at[7])
        took(r4_v.at[pl.ds(0, NS - 1)], ssem.at[8])

    @pl.when(jnp.logical_not(mine))
    def _():
        took(r2_v.at[pl.ds(0, OWN)], ssem.at[1])
        took(r4_v.at[pl.ds(0, OWN)], ssem.at[3])
        took(r7_v.at[pl.ds(0, OWN)], ssem.at[7])

    o_key.wait()
    o_val.wait()
    o_upd.wait()


def per_device(
    hidden,
    token_index_list,
    embedding,
    attention_gain,
    query_key_value_matrix,
    attention_adapter_down,
    attention_adapter_up,
    cached_key_rows,
    cached_value_rows,
    lengths,
    output_matrix,
    feedforward_gain,
    gate_matrix,
    up_matrix,
    feedforward_adapter_down,
    feedforward_adapter_up,
    down_matrix,
):
    hbm = pl.BlockSpec(memory_space=pl.ANY)
    vm = pltpu.VMEM
    return pl.pallas_call(
        kernel,
        name="block",
        out_shape=(
            jax.ShapeDtypeStruct((REQ, TOK, F), BF),
            jax.ShapeDtypeStruct((REQ, TOK, CW), BF),
            jax.ShapeDtypeStruct((REQ, TOK, CW), BF),
        ),
        in_specs=[hbm] * 17,
        out_specs=(hbm, hbm, hbm),
        scratch_shapes=[
            vm((TOK, REQ), jnp.int32),
            pltpu.SMEM((REQ,), jnp.int32),
            vm((REQ, TOK, F), BF),
            vm((F, VR), BF),
            vm((2, F), BF),
            vm((3, 2 * FP, CW), BF),
            vm((2 * FP, 128), BF),
            vm((3, 128, CW), BF),
            vm((REQ, POS, CW), BF),
            vm((REQ, POS, CW), BF),
            vm((FP, CW), BF),
            vm((1, F), BF),
            vm((FP, UW), BF),
            vm((FP, UW), BF),
            vm((FP, 128), BF),
            vm((128, 2, UW), BF),
            vm((2, 128, UW), BF),
            vm((FP, UW), BF),
            vm((ROWS, FP), F32),
            vm((NM, ROWS, FP), BF),
            vm((NJ, ROWS, 512), BF),
            vm((NS, RT, 512), BF),
            vm((NJ, ROWS, 384), BF),
            vm((NI, HEADS * RT, CW), BF),
            vm((NJ, ROWS, 256), BF),
            vm((NS, RT, 256), BF),
            vm((ROWS, CW), BF),
            vm((ROWS, FP), F32),
            vm((NM, 8, FP), F32),
            vm((ROWS, FP), F32),
            vm((NJ, ROWS, 640), BF),
            vm((NS, RT, 640), BF),
            vm((ROWS, UW), BF),
            vm((ROWS, FP), F32),
            vm((NM, 8, FP), F32),
            vm((ROWS, FP), F32),
            vm((REQ, TOK, F), BF),
            vm((REQ, TOK, CW), BF),
            vm((REQ, TOK, CW), BF),
            pltpu.SemaphoreType.DMA((24,)),
            pltpu.SemaphoreType.DMA((11,)),
            pltpu.SemaphoreType.DMA((11,)),
        ],
        compiler_params=pltpu.CompilerParams(
            collective_id=0, has_side_effects=True, vmem_limit_bytes=56 * 1024 * 1024
        ),
    )(
        token_index_list.T,
        lengths,
        hidden,
        embedding.T,
        attention_gain,
        jnp.transpose(query_key_value_matrix, (0, 2, 1, 3)),
        attention_adapter_down,
        jnp.transpose(attention_adapter_up, (1, 0, 2)),
        cached_key_rows,
        cached_value_rows,
        output_matrix.T,
        feedforward_gain.reshape(1, F),
        gate_matrix,
        up_matrix,
        feedforward_adapter_down,
        feedforward_adapter_up,
        down_matrix.T,
    )


def solution(mesh):
    placed = (
        P(None, None, "seq"),
        P(),
        P("mp", "seq"),
        P(None, "seq"),
        P(None, "seq", None, "mp"),
        P(None, "seq", None),
        P(None, None, "mp"),
        P(None, "seq", "mp"),
        P(None, "seq", "mp"),
        P(),
        P("mp", "seq"),
        P("seq"),
        P("seq", "mp"),
        P("seq", "mp"),
        P("seq", None),
        P(None, None, "mp"),
        P("mp", "seq"),
    )
    return jax.shard_map(
        per_device,
        mesh=mesh,
        in_specs=placed,
        out_specs=(P(None, None, "seq"), P(None, None, "mp"), P(None, None, "mp")),
        check_vma=False,
    )
```

```python
import jax
import jax.numpy as jnp
from jax import lax
from jax.experimental import pallas as pl
from jax.experimental.pallas import tpu as pltpu
from jax.sharding import PartitionSpec as P

MODEL_WIDTH = 3584
HEAD_DIM = 224
EPS = 1e-05
DEAD = -1e30

NS = 32
NM = 8
ROWS = 64
F = 112
FP = 128
CW = 896
HEADS = 4
UW = 1792
POS = 128
VR = 4000
REQ = 16
TOK = 4
RT = 16
NI = ROWS // RT
NJ = 7
OWN = NI * NJ

def hops(offset):
    dx, dy, dc = offset
    return min(dx, 4 - dx) + min(dy, 4 - dy)


SEQ_ORDER = sorted(
    ((dx, dy, dc) for dx in range(4) for dy in range(4) for dc in range(2) if dx or dy or dc),
    key=lambda offset: -hops(offset),
)
MP_ORDER = (4, 3, 5, 2, 6, 1, 7)

BF = jnp.bfloat16
F32 = jnp.float32
MESH = pl.DeviceIdType.MESH

DIMS_NT = (((1,), (1,)), ((), ()))


def mm(a, b):
    return jnp.dot(a, b, preferred_element_type=F32)


def mm_nt(a, b):
    return lax.dot_general(a, b, DIMS_NT, preferred_element_type=F32)


def head_of(col):
    one = jnp.int32(1)
    zero = jnp.int32(0)
    return (
        jnp.where(col >= HEAD_DIM, one, zero)
        + jnp.where(col >= 2 * HEAD_DIM, one, zero)
        + jnp.where(col >= 3 * HEAD_DIM, one, zero)
    )


def kernel(
    ids_hbm,
    len_hbm,
    hid_hbm,
    emb_hbm,
    gain_hbm,
    wqkv_hbm,
    adown_hbm,
    aup_hbm,
    kc_hbm,
    vc_hbm,
    wout_hbm,
    fgain_hbm,
    gate_hbm,
    upm_hbm,
    fdown_hbm,
    fup_hbm,
    down_hbm,
    upd_v,
    key_v,
    val_v,
    ids_v,
    len_s,
    hid_v,
    emb_v,
    gain_v,
    wq_v,
    ad_v,
    aup_v,
    kc_v,
    vc_v,
    wo_v,
    fgain_v,
    gate_v,
    upm_v,
    fd_v,
    fup_v,
    fu_v,
    dn_v,
    h_v,
    ph_v,
    es_v,
    s2_v,
    r2_v,
    s2k_v,
    r2k_v,
    gq_v,
    g_v,
    qm_v,
    s4_v,
    r4_v,
    a_v,
    hr_v,
    mid_v,
    x7_v,
    p7_v,
    s7_v,
    r7_v,
    a2_v,
    dr_v,
    lsem,
    ssem,
    rsem,
):
    me_s = lax.axis_index("seq")
    me_m = lax.axis_index("mp")
    mine = me_s < OWN
    my_i = lax.div(me_s, NJ)
    my_j = lax.rem(me_s, NJ)
    my_i = jnp.where(mine, my_i, 0)
    my_j = jnp.where(mine, my_j, 0)
    my_rows = pl.ds(pl.multiple_of(my_i * RT, RT), RT)

    barrier = pltpu.get_barrier_semaphore()

    x = lax.div(me_s, 8)
    y = lax.rem(lax.div(me_s, 2), 4)
    core = lax.rem(me_s, 2)

    def each_seq(fn):
        for dx, dy, dc in SEQ_ORDER:
            px = lax.rem(x + dx, 4) if dx else x
            py = lax.rem(y + dy, 4) if dy else y
            pc = 1 - core if dc else core
            fn((px * 4 + py) * 2 + pc)

    def each_mp(fn):
        for d in MP_ORDER:
            fn(lax.rem(me_m + d, NM))

    def greet(axis):
        def fn(p):
            pl.semaphore_signal(barrier, inc=1, device_id={axis: p}, device_id_type=MESH)

        return fn

    each_mp(greet("mp"))
    each_seq(greet("seq"))

    local = []

    def fetch(src, dst):
        copy = pltpu.make_async_copy(src, dst, lsem.at[len(local)])
        copy.start()
        local.append(copy)
        return copy

    c_ids = fetch(ids_hbm, ids_v)
    c_emb = fetch(emb_hbm, emb_v)
    c_hid = fetch(hid_hbm, hid_v)
    c_gain = fetch(gain_hbm, gain_v)
    c_ad0 = fetch(adown_hbm.at[0], ad_v.at[pl.ds(0, F)])
    c_ad1 = fetch(adown_hbm.at[1], ad_v.at[pl.ds(FP, F)])
    c_wq0 = fetch(wqkv_hbm.at[0], wq_v.at[:, pl.ds(0, F)])
    c_wq1 = fetch(wqkv_hbm.at[1], wq_v.at[:, pl.ds(FP, F)])
    c_aup = fetch(aup_hbm, aup_v)
    c_len = fetch(len_hbm, len_s)
    c_kc = fetch(kc_hbm, kc_v)
    c_vc = fetch(vc_hbm, vc_v)
    c_wo = fetch(wout_hbm, wo_v.at[pl.ds(0, F)])
    c_fg = fetch(fgain_hbm, fgain_v)
    c_fup = fetch(fup_hbm, fup_v)
    c_fd = fetch(fdown_hbm, fd_v.at[pl.ds(0, F)])
    c_gate = fetch(gate_hbm, gate_v.at[pl.ds(0, F)])
    c_upm = fetch(upm_hbm, upm_v.at[pl.ds(0, F)])
    c_dn = fetch(down_hbm, dn_v.at[pl.ds(0, F)])

    pad = FP - F
    wq_v[:, pl.ds(F, pad), :] = jnp.zeros((3, pad, CW), BF)
    wq_v[:, pl.ds(FP + F, pad), :] = jnp.zeros((3, pad, CW), BF)
    ad_v[pl.ds(F, pad), :] = jnp.zeros((pad, FP), BF)
    ad_v[pl.ds(FP + F, pad), :] = jnp.zeros((pad, FP), BF)
    wo_v[pl.ds(F, pad), :] = jnp.zeros((pad, CW), BF)
    fd_v[pl.ds(F, pad), :] = jnp.zeros((pad, FP), BF)
    gate_v[pl.ds(F, pad), :] = jnp.zeros((pad, UW), BF)
    upm_v[pl.ds(F, pad), :] = jnp.zeros((pad, UW), BF)
    dn_v[pl.ds(F, pad), :] = jnp.zeros((pad, UW), BF)
    h_v[...] = jnp.zeros((ROWS, FP), F32)

    def took(ref, sem):
        pltpu.make_async_copy(ref, ref, sem).wait()

    def send(src, dst, phase, axis, p):
        pltpu.make_async_remote_copy(
            src_ref=src,
            dst_ref=dst,
            send_sem=ssem.at[phase],
            recv_sem=rsem.at[phase],
            device_id={axis: p},
            device_id_type=MESH,
        ).start()

    def scatter(src_of, dst, phase):
        def fn(p):
            @pl.when(p < OWN)
            def _():
                send(src_of(lax.div(p, NJ), lax.rem(p, NJ)), dst, phase, "seq", p)

        each_seq(fn)

    def gather(ref, phase):
        each_seq(lambda p: send(ref, ref, phase, "seq", p))

    c_ids.wait()
    ids = ids_v[...]
    high = ids // 256
    low = ids - high * 256
    spread = (
        lax.broadcasted_iota(jnp.int32, (REQ, ROWS), 0)
        == lax.broadcasted_iota(jnp.int32, (REQ, ROWS), 1) // TOK
    ).astype(F32).astype(BF)
    wide = mm(high.astype(F32).astype(BF), spread) * 256.0 + mm(low.astype(F32).astype(BF), spread)
    pick = lax.broadcasted_iota(jnp.int32, (TOK, ROWS), 0) == (
        lax.broadcasted_iota(jnp.int32, (TOK, ROWS), 1) % TOK
    )
    id_row = jnp.sum(jnp.where(pick, wide, 0.0), 0, keepdims=True).astype(jnp.int32)
    id_row = id_row - me_m * VR
    selector = (
        (lax.broadcasted_iota(jnp.int32, (VR, ROWS), 0) == id_row).astype(F32).astype(BF)
    )
    c_emb.wait()
    found = mm(emb_v[...], selector)
    found = jnp.concatenate([found, jnp.zeros((pad, ROWS), F32)], 0)
    es_v[me_m] = found.T.astype(BF)

    pl.semaphore_wait(barrier, NS + NM - 2)

    each_mp(lambda p: send(es_v.at[me_m], es_v.at[me_m], 0, "mp", p))

    c_hid.wait()
    c_gain.wait()
    for b in range(REQ):
        h_v[pl.ds(TOK * b, TOK), pl.ds(0, F)] = hid_v[b].astype(F32)
    gains = gain_v[...].astype(F32)
    gains = jnp.concatenate([gains, jnp.zeros((2, pad), F32)], 1)
    state = h_v[...]
    scaled_h = (state * gains[0:1]).astype(BF)
    c_ad0.wait()
    c_ad1.wait()
    c_aup.wait()
    c_wq0.wait()
    c_wq1.wait()
    low_h = mm(scaled_h, ad_v[pl.ds(0, FP), :]).astype(BF)
    low_w = ad_v[pl.ds(FP, FP), :]
    for part in range(3):
        ph_v[part] = mm(scaled_h, wq_v[part, pl.ds(0, FP), :]) + mm(low_h, aup_v[part])
        wq_v[part, pl.ds(FP, FP), :] = (
            wq_v[part, pl.ds(FP, FP), :].astype(F32) + mm(low_w, aup_v[part])
        ).astype(BF)
    squares_h = jnp.sum(state * state, 1, keepdims=True)

    took(es_v.at[pl.ds(0, NM - 1)], rsem.at[0])
    embed = es_v[0].astype(F32)
    for q in range(1, NM):
        embed = embed + es_v[q].astype(F32)
    scaled_e = (embed * gains[1:2]).astype(BF)
    squares = squares_h + jnp.sum(embed * embed, 1, keepdims=True)
    squares = jnp.broadcast_to(squares, (ROWS, 128)).astype(BF)

    def project(part, dst, at):
        proj = (ph_v[part] + mm(scaled_e, wq_v[part, pl.ds(FP, FP), :])).astype(BF)
        for j in range(NJ):
            dst[j, :, pl.ds(at, 128)] = proj[:, 128 * j : 128 * j + 128]

    def block_of(ref):
        return lambda i, j: ref.at[j, pl.ds(pl.multiple_of(i * RT, RT), RT)]

    for j in range(NJ):
        s2_v[j, :, pl.ds(128, 128)] = squares
    project(0, s2_v, 0)
    scatter(block_of(s2_v), r2_v.at[me_s], 1)
    project(1, s2k_v, 0)
    project(2, s2k_v, 128)
    scatter(block_of(s2k_v), r2k_v.at[me_s], 2)
    my_cols = pl.ds(pl.multiple_of(my_j * 128, 128), 128)

    @pl.when(mine)
    def _():
        r2_v[me_s] = s2_v[my_j, my_rows, :]
        r2k_v[me_s] = s2k_v[my_j, my_rows, :]
        took(r2_v.at[pl.ds(0, NS - 1)], rsem.at[1])
        total = r2_v[0].astype(F32)
        for s in range(1, NS):
            total = total + r2_v[s].astype(F32)
        scale = 1.0 / jnp.sqrt(total[:, 128:] / (2 * MODEL_WIDTH) + EPS)
        block = gq_v.at[my_rows, my_cols]
        block[...] = (total[:, :128] * scale).astype(BF)
        gather(block, 3)
        took(r2k_v.at[pl.ds(0, NS - 1)], rsem.at[2])
        total = r2k_v[0].astype(F32)
        for s in range(1, NS):
            total = total + r2k_v[s].astype(F32)
        scale = jnp.concatenate([scale, scale], 1)
        g_v[my_j, my_rows, :] = (total * scale).astype(BF)
        gather(g_v.at[my_j, my_rows], 4)
        took(r2_v.at[pl.ds(0, OWN - 1), :, pl.ds(0, 128)], rsem.at[3])

    @pl.when(jnp.logical_not(mine))
    def _():
        took(r2_v.at[pl.ds(0, OWN), :, pl.ds(0, 128)], rsem.at[3])

    lane = lax.broadcasted_iota(jnp.int32, (RT, 128), 1)
    for i in range(NI):
        rows = pl.ds(RT * i, RT)
        for c in range(NJ):
            q = gq_v[rows, pl.ds(128 * c, 128)].astype(F32)
            first, last = (128 * c) // HEAD_DIM, (128 * c + 127) // HEAD_DIM
            for h in range(HEADS):
                if first == last == h:
                    part = q
                elif h in (first, last):
                    part = jnp.where(head_of(lane + 128 * c) == h, q, 0.0)
                else:
                    part = jnp.zeros((RT, 128), F32)
                qm_v[i, pl.ds(RT * h, RT), pl.ds(128 * c, 128)] = part.astype(BF)

    inv_scale = 1.0 / (HEAD_DIM**0.5)
    c_len.wait()
    c_kc.wait()
    c_vc.wait()
    place = me_s * POS + lax.broadcasted_iota(jnp.int32, (HEADS * RT, POS), 1)
    group = (lax.broadcasted_iota(jnp.int32, (HEADS * RT, POS), 0) % RT) // TOK
    for i in range(NI):
        score = jnp.full((HEADS * RT, POS), DEAD, F32)
        for k in range(RT // TOK):
            b = (RT // TOK) * i + k
            one = mm_nt(qm_v[i], kc_v[b]) * inv_scale
            score = jnp.where((group == k) & (place < len_s[b]), one, score)
        peak = jnp.max(score, 1, keepdims=True)
        weight = jnp.where(score > 0.5 * DEAD, jnp.exp(score - peak), 0.0)
        total = jnp.sum(weight, 1, keepdims=True)
        spread_w = jnp.concatenate(
            [jnp.where(group == k, weight, 0.0).astype(BF) for k in range(RT // TOK)], 1
        )
        values = vc_v[pl.ds((RT // TOK) * i, RT // TOK)].reshape((RT // TOK) * POS, CW)
        numer = mm(spread_w, values)
        live = total > 0.0
        safe = jnp.where(live, total, 1.0)
        lse = jnp.where(live, peak + jnp.log(safe), DEAD)
        inverse = 1.0 / safe
        stats = jnp.zeros((RT, 128), F32)
        for h in range(HEADS):
            rest = jnp.broadcast_to(lse[RT * h : RT * h + RT], (RT, 128))
            for piece in range(3):
                lead = rest.astype(BF).astype(F32)
                stats = jnp.where(lane == 3 * h + piece, lead, stats)
                rest = rest - lead
        stats = stats.astype(BF)
        rows = pl.ds(RT * i, RT)
        for c in range(NJ):
            first, last = (128 * c) // HEAD_DIM, (128 * c + 127) // HEAD_DIM
            cols = slice(128 * c, 128 * c + 128)
            here = numer[RT * first : RT * first + RT, cols] * inverse[RT * first : RT * first + RT]
            if last != first:
                there = numer[RT * last : RT * last + RT, cols] * inverse[RT * last : RT * last + RT]
                here = jnp.where(head_of(lane + 128 * c) == first, here, there)
            s4_v[c, rows, pl.ds(0, 128)] = here.astype(BF)
            s4_v[c, rows, pl.ds(128, 128)] = stats

    scatter(block_of(s4_v), r4_v.at[me_s], 5)

    @pl.when(mine)
    def _():
        took(r2_v.at[pl.ds(0, OWN - 1)], rsem.at[4])

    @pl.when(jnp.logical_not(mine))
    def _():
        took(r2_v.at[pl.ds(0, OWN)], rsem.at[4])

    @pl.when(mine)
    def _():
        r4_v[me_s] = s4_v[my_j, my_rows, :]
        lane_head = head_of(lane + 128 * my_j)
        head_a = head_of(128 * my_j)
        head_b = head_of(128 * my_j + 127)
        q = gq_v[my_rows, :].astype(F32)
        k = jnp.concatenate([g_v[c, my_rows, pl.ds(0, 128)] for c in range(NJ)], 1)
        v = g_v[my_j, my_rows, pl.ds(128, 128)]
        col_head = head_of(lax.broadcasted_iota(jnp.int32, (RT, CW), 1))
        r_at = lax.broadcasted_iota(jnp.int32, (RT, RT), 0)
        c_at = lax.broadcasted_iota(jnp.int32, (RT, RT), 1)
        seen = (r_at // TOK == c_at // TOK) & (c_at % TOK <= r_at % TOK)

        def fresh(head):
            score = mm_nt(jnp.where(col_head == head, q, 0.0).astype(BF), k) * inv_scale
            score = jnp.where(seen, score, DEAD)
            peak = jnp.max(score, 1, keepdims=True)
            weight = jnp.where(seen, jnp.exp(score - peak), 0.0)
            total = jnp.sum(weight, 1, keepdims=True)
            return mm(weight.astype(BF), v) / total, peak + jnp.log(total)

        out_a, lse_a = fresh(head_a)
        out_b, lse_b = fresh(head_b)
        new_out = jnp.where(lane_head == head_a, out_a, out_b)
        new_lse = jnp.where(lane_head == head_a, lse_a, lse_b)

        stat_head = lax.broadcasted_iota(jnp.int32, (128, 128), 0) // 3
        expand = (
            (stat_head == head_of(lax.broadcasted_iota(jnp.int32, (128, 128), 1) + 128 * my_j))
            .astype(F32)
            .astype(BF)
        )
        took(r4_v.at[pl.ds(0, NS - 1)], rsem.at[5])
        stats = r4_v[:, :, pl.ds(128, 128)].reshape(NS * RT, 128)
        lse = mm(stats, expand).reshape(NS, RT, 128)
        peak = jnp.maximum(jnp.max(lse, 0), new_lse)
        weight = jnp.exp(lse - peak[None])
        new_weight = jnp.exp(new_lse - peak)
        total = jnp.sum(weight, 0) + new_weight
        numer = jnp.sum(weight * r4_v[:, :, pl.ds(0, 128)].astype(F32), 0) + new_weight * new_out
        block = a_v.at[my_rows, my_cols]
        block[...] = (numer / total).astype(BF)
        gather(block, 6)

    for b in range(REQ):
        for c in range(NJ):
            key_v[b, :, pl.ds(128 * c, 128)] = g_v[c, pl.ds(TOK * b, TOK), pl.ds(0, 128)]
            val_v[b, :, pl.ds(128 * c, 128)] = g_v[c, pl.ds(TOK * b, TOK), pl.ds(128, 128)]
    c_fup.wait()

    def split(k, carry):
        at = pl.ds(pl.multiple_of(k * 16, 16), 16)
        two = fup_v[at].astype(F32)
        fu_v[0, at, :] = two[:, 0, :].astype(BF)
        fu_v[1, at, :] = two[:, 1, :].astype(BF)
        return carry

    lax.fori_loop(0, 8, split, 0)
    c_fg.wait()
    c_fd.wait()
    c_gate.wait()
    c_upm.wait()
    for part, w_v in enumerate((gate_v, upm_v)):
        w_v[...] = (w_v[...].astype(F32) + mm(fd_v[...], fu_v[part])).astype(BF)
    c_wo.wait()

    @pl.when(mine)
    def _():
        took(r4_v.at[pl.ds(0, OWN - 1), :, pl.ds(0, 128)], rsem.at[6])

    @pl.when(jnp.logical_not(mine))
    def _():
        took(r4_v.at[pl.ds(0, OWN), :, pl.ds(0, 128)], rsem.at[6])

    def sum_mp(part, slot_v, phase, meanwhile=lambda: None):
        slot_v[me_m] = part.astype(BF)
        each_mp(lambda p: send(slot_v.at[me_m], slot_v.at[me_m], phase, "mp", p))
        meanwhile()
        took(slot_v.at[pl.ds(0, NM - 1)], rsem.at[phase])
        total = slot_v[0].astype(F32)
        for q in range(1, NM):
            total = total + slot_v[q].astype(F32)
        return total

    mixed = sum_mp(mm_nt(a_v[...], wo_v[...]), hr_v, 7)
    mid_v[...] = mixed + h_v[...]
    fgain = jnp.concatenate([fgain_v[...].astype(F32), jnp.zeros((1, pad), F32)], 1)

    mid = mid_v[...]
    scaled_m = (mid * fgain).astype(BF)
    squares = jnp.broadcast_to(jnp.sum(mid * mid, 1, keepdims=True), (ROWS, 128))

    def partial(j):
        at = pl.ds(pl.multiple_of(j * 256, 256), 256)
        return jnp.concatenate(
            [mm(scaled_m, gate_v[:, at]), mm(scaled_m, upm_v[:, at]), squares], 1
        )

    sibling = me_s + 1 - 2 * core
    for k in range(4):
        x7_v[0, k] = partial(3 * (1 - core) + k).astype(BF)
    send(x7_v.at[0], x7_v.at[1], 11, "seq", sibling)
    for k in range(4):
        p7_v[k] = partial(3 * core + k)
    took(x7_v.at[1], rsem.at[11])
    for k in range(4):
        s7_v[k] = (p7_v[k] + x7_v[1, k].astype(F32)).astype(BF)

    def sent_here(i, j):
        upper = jnp.where(i >= NI // 2, 1, 0)
        return jnp.where(j < 3, 0, jnp.where(j > 3, 1, upper)) == core

    def block7(i, j):
        return s7_v.at[j - 3 * core, pl.ds(pl.multiple_of(i * RT, RT), RT)]

    def send7(p):
        i, j = lax.div(p, NJ), lax.rem(p, NJ)

        @pl.when((p < OWN) & sent_here(i, j))
        def _():
            send(block7(i, j), r7_v.at[lax.div(me_s, 2)], 8, "seq", p)

    each_seq(send7)
    own_block = mine & sent_here(my_i, my_j)

    @pl.when(mine)
    def _():
        @pl.when(own_block)
        def _():
            r7_v[lax.div(me_s, 2)] = s7_v[my_j - 3 * core, my_rows, :]
            took(r7_v.at[pl.ds(0, NS // 2 - 1)], rsem.at[8])

        @pl.when(jnp.logical_not(own_block))
        def _():
            took(r7_v.at[pl.ds(0, NS // 2)], rsem.at[8])

        total = r7_v[0].astype(F32)
        for s in range(1, NS // 2):
            total = total + r7_v[s].astype(F32)
        scale = 1.0 / jnp.sqrt(total[:, 512:] / MODEL_WIDTH + EPS)
        scale = jnp.concatenate([scale, scale], 1)
        gate = total[:, 0:256] * scale
        up = total[:, 256:512] * scale
        block = a2_v.at[my_rows, pl.ds(pl.multiple_of(my_j * 256, 256), 256)]
        block[...] = (jax.nn.gelu(gate, approximate=True) * up).astype(BF)
        gather(block, 9)
        took(r4_v.at[pl.ds(0, OWN - 1)], rsem.at[9])

    @pl.when(jnp.logical_not(mine))
    def _():
        took(r4_v.at[pl.ds(0, OWN)], rsem.at[9])

    c_dn.wait()
    down = sum_mp(mm_nt(a2_v[...], dn_v[...]), dr_v, 10)
    updated = (down + mid_v[...]).astype(BF)
    for b in range(REQ):
        upd_v[b] = updated[TOK * b : TOK * b + TOK, :F]

    took(es_v.at[pl.ds(0, NM - 1)], ssem.at[0])
    took(hr_v.at[pl.ds(0, NM - 1)], ssem.at[7])
    took(dr_v.at[pl.ds(0, NM - 1)], ssem.at[10])
    took(x7_v.at[1], ssem.at[11])

    @pl.when(own_block)
    def _():
        took(r7_v.at[pl.ds(0, OWN // 2 - 1)], ssem.at[8])

    @pl.when(jnp.logical_not(own_block))
    def _():
        took(r7_v.at[pl.ds(0, OWN // 2)], ssem.at[8])

    @pl.when(mine)
    def _():
        took(r2_v.at[pl.ds(0, OWN - 1)], ssem.at[1])
        took(r2k_v.at[pl.ds(0, OWN - 1)], ssem.at[2])
        took(r2_v.at[pl.ds(0, NS - 1), :, pl.ds(0, 128)], ssem.at[3])
        took(r2_v.at[pl.ds(0, NS - 1)], ssem.at[4])
        took(r4_v.at[pl.ds(0, OWN - 1)], ssem.at[5])
        took(r4_v.at[pl.ds(0, NS - 1), :, pl.ds(0, 128)], ssem.at[6])
        took(r4_v.at[pl.ds(0, NS - 1)], ssem.at[9])

    @pl.when(jnp.logical_not(mine))
    def _():
        took(r2_v.at[pl.ds(0, OWN)], ssem.at[1])
        took(r2k_v.at[pl.ds(0, OWN)], ssem.at[2])
        took(r4_v.at[pl.ds(0, OWN)], ssem.at[5])


def per_device(
    hidden,
    token_index_list,
    embedding,
    attention_gain,
    query_key_value_matrix,
    attention_adapter_down,
    attention_adapter_up,
    cached_key_rows,
    cached_value_rows,
    lengths,
    output_matrix,
    feedforward_gain,
    gate_matrix,
    up_matrix,
    feedforward_adapter_down,
    feedforward_adapter_up,
    down_matrix,
):
    hbm = pl.BlockSpec(memory_space=pl.ANY)
    inner = pl.BlockSpec(memory_space=pltpu.VMEM)
    vm = pltpu.VMEM
    return pl.pallas_call(
        kernel,
        name="block",
        out_shape=(vm((REQ, TOK, F), BF), vm((REQ, TOK, CW), BF), vm((REQ, TOK, CW), BF)),
        in_specs=[hbm] * 17,
        out_specs=(inner, inner, inner),
        scratch_shapes=[
            vm((TOK, REQ), jnp.int32),
            pltpu.SMEM((REQ,), jnp.int32),
            vm((REQ, TOK, F), BF),
            vm((F, VR), BF),
            vm((2, F), BF),
            vm((3, 2 * FP, CW), BF),
            vm((2 * FP, 128), BF),
            vm((3, 128, CW), BF),
            vm((REQ, POS, CW), BF),
            vm((REQ, POS, CW), BF),
            vm((FP, CW), BF),
            vm((1, F), BF),
            vm((FP, UW), BF),
            vm((FP, UW), BF),
            vm((FP, 128), BF),
            vm((128, 2, UW), BF),
            vm((2, 128, UW), BF),
            vm((FP, UW), BF),
            vm((ROWS, FP), F32),
            vm((3, ROWS, CW), F32),
            vm((NM, ROWS, FP), BF),
            vm((NJ, ROWS, 256), BF),
            vm((NS, RT, 256), BF),
            vm((NJ, ROWS, 256), BF),
            vm((NS, RT, 256), BF),
            vm((ROWS, CW), BF),
            vm((NJ, ROWS, 256), BF),
            vm((NI, HEADS * RT, CW), BF),
            vm((NJ, ROWS, 256), BF),
            vm((NS, RT, 256), BF),
            vm((ROWS, CW), BF),
            vm((NM, ROWS, FP), BF),
            vm((ROWS, FP), F32),
            vm((2, 4, ROWS, 640), BF),
            vm((4, ROWS, 640), F32),
            vm((4, ROWS, 640), BF),
            vm((NS // 2, RT, 640), BF),
            vm((ROWS, UW), BF),
            vm((NM, ROWS, FP), BF),
            pltpu.SemaphoreType.DMA((24,)),
            pltpu.SemaphoreType.DMA((12,)),
            pltpu.SemaphoreType.DMA((12,)),
        ],
        compiler_params=pltpu.CompilerParams(
            collective_id=0, has_side_effects=True, vmem_limit_bytes=56 * 1024 * 1024
        ),
    )(
        token_index_list.T,
        lengths,
        hidden,
        embedding.T,
        attention_gain,
        jnp.transpose(query_key_value_matrix, (0, 2, 1, 3)),
        attention_adapter_down,
        jnp.transpose(attention_adapter_up, (1, 0, 2)),
        cached_key_rows,
        cached_value_rows,
        output_matrix.T,
        feedforward_gain.reshape(1, F),
        gate_matrix,
        up_matrix,
        feedforward_adapter_down,
        feedforward_adapter_up,
        down_matrix.T,
    )


def solution(mesh):
    placed = (
        P(None, None, "seq"),
        P(),
        P("mp", "seq"),
        P(None, "seq"),
        P(None, "seq", None, "mp"),
        P(None, "seq", None),
        P(None, None, "mp"),
        P(None, "seq", "mp"),
        P(None, "seq", "mp"),
        P(),
        P("mp", "seq"),
        P("seq"),
        P("seq", "mp"),
        P("seq", "mp"),
        P("seq", None),
        P(None, None, "mp"),
        P("mp", "seq"),
    )
    return jax.shard_map(
        per_device,
        mesh=mesh,
        in_specs=placed,
        out_specs=(P(None, None, "seq"), P(None, None, "mp"), P(None, None, "mp")),
        check_vma=False,
    )
```

```python
import jax
import jax.numpy as jnp
from jax import lax
from jax.experimental import pallas as pl
from jax.experimental.pallas import tpu as pltpu
from jax.sharding import PartitionSpec as P

MODEL_WIDTH = 3584
HEAD_DIM = 224
EPS = 1e-05
DEAD = -1e30

NS = 32
NM = 8
ROWS = 64
F = 112
FP = 128
CW = 896
HEADS = 4
UW = 1792
POS = 128
VR = 4000
REQ = 16
TOK = 4
RT = 16
NI = ROWS // RT
NJ = 7
OWN = NI * NJ

def hops(offset):
    dx, dy, dc = offset
    return min(dx, 4 - dx) + min(dy, 4 - dy)


SEQ_ORDER = sorted(
    ((dx, dy, dc) for dx in range(4) for dy in range(4) for dc in range(2) if dx or dy or dc),
    key=lambda offset: (-hops(offset), offset[2]),
)
MP_ORDER = (4, 3, 5, 2, 6, 1, 7)

BF = jnp.bfloat16
F32 = jnp.float32
MESH = pl.DeviceIdType.MESH

DIMS_NT = (((1,), (1,)), ((), ()))


def mm(a, b):
    return jnp.dot(a, b, preferred_element_type=F32)


def mm_nt(a, b):
    return lax.dot_general(a, b, DIMS_NT, preferred_element_type=F32)


def head_of(col):
    one = jnp.int32(1)
    zero = jnp.int32(0)
    return (
        jnp.where(col >= HEAD_DIM, one, zero)
        + jnp.where(col >= 2 * HEAD_DIM, one, zero)
        + jnp.where(col >= 3 * HEAD_DIM, one, zero)
    )


def kernel(
    ids_hbm,
    len_hbm,
    hid_hbm,
    emb_hbm,
    gain_hbm,
    wqkv_hbm,
    adown_hbm,
    aup_hbm,
    kc_hbm,
    vc_hbm,
    wout_hbm,
    fgain_hbm,
    gate_hbm,
    upm_hbm,
    fdown_hbm,
    fup_hbm,
    down_hbm,
    upd_v,
    key_v,
    val_v,
    ids_v,
    len_s,
    hid_v,
    emb_v,
    gain_v,
    wq_v,
    ad_v,
    aup_v,
    kc_v,
    vc_v,
    wo_v,
    fgain_v,
    gate_v,
    upm_v,
    fd_v,
    fup_v,
    fu_v,
    dn_v,
    h_v,
    ph_v,
    es_v,
    s2_v,
    r2_v,
    s2k_v,
    r2k_v,
    gq_v,
    g_v,
    qm_v,
    s4_v,
    r4_v,
    a_v,
    scale_v,
    hr_v,
    mid_v,
    x7_v,
    p7_v,
    s7_v,
    r7_v,
    a2_v,
    dr_v,
    lsem,
    ssem,
    rsem,
):
    me_s = lax.axis_index("seq")
    me_m = lax.axis_index("mp")
    mine = me_s < OWN
    my_i = lax.div(me_s, NJ)
    my_j = lax.rem(me_s, NJ)
    my_i = jnp.where(mine, my_i, 0)
    my_j = jnp.where(mine, my_j, 0)
    my_rows = pl.ds(pl.multiple_of(my_i * RT, RT), RT)

    barrier = pltpu.get_barrier_semaphore()

    x = lax.div(me_s, 8)
    y = lax.rem(lax.div(me_s, 2), 4)
    core = lax.rem(me_s, 2)

    def each_seq(fn):
        for dx, dy, dc in SEQ_ORDER:
            px = lax.rem(x + dx, 4) if dx else x
            py = lax.rem(y + dy, 4) if dy else y
            pc = 1 - core if dc else core
            fn((px * 4 + py) * 2 + pc)

    def each_mp(fn):
        for d in MP_ORDER:
            fn(lax.rem(me_m + d, NM))

    def greet(axis):
        def fn(p):
            pl.semaphore_signal(barrier, inc=1, device_id={axis: p}, device_id_type=MESH)

        return fn

    each_mp(greet("mp"))
    each_seq(greet("seq"))

    local = []

    def fetch(src, dst):
        copy = pltpu.make_async_copy(src, dst, lsem.at[len(local)])
        copy.start()
        local.append(copy)
        return copy

    c_ids = fetch(ids_hbm, ids_v)
    c_emb = fetch(emb_hbm, emb_v)
    c_hid = fetch(hid_hbm, hid_v)
    c_gain = fetch(gain_hbm, gain_v)

    pad = FP - F
    wq_v[:, pl.ds(F, pad), :] = jnp.zeros((3, pad, CW), BF)
    wq_v[:, pl.ds(FP + F, pad), :] = jnp.zeros((3, pad, CW), BF)
    ad_v[pl.ds(F, pad), :] = jnp.zeros((pad, FP), BF)
    ad_v[pl.ds(FP + F, pad), :] = jnp.zeros((pad, FP), BF)
    wo_v[pl.ds(F, pad), :] = jnp.zeros((pad, CW), BF)
    fd_v[pl.ds(F, pad), :] = jnp.zeros((pad, FP), BF)
    gate_v[pl.ds(F, pad), :] = jnp.zeros((pad, UW), BF)
    upm_v[pl.ds(F, pad), :] = jnp.zeros((pad, UW), BF)
    dn_v[pl.ds(F, pad), :] = jnp.zeros((pad, UW), BF)
    h_v[...] = jnp.zeros((ROWS, FP), F32)

    def took(ref, sem):
        pltpu.make_async_copy(ref, ref, sem).wait()

    def send(src, dst, phase, axis, p):
        pltpu.make_async_remote_copy(
            src_ref=src,
            dst_ref=dst,
            send_sem=ssem.at[phase],
            recv_sem=rsem.at[phase],
            device_id={axis: p},
            device_id_type=MESH,
        ).start()

    def scatter(src_of, dst, phase):
        def fn(p):
            @pl.when(p < OWN)
            def _():
                send(src_of(lax.div(p, NJ), lax.rem(p, NJ)), dst, phase, "seq", p)

        each_seq(fn)

    def gather(ref, phase):
        each_seq(lambda p: send(ref, ref, phase, "seq", p))

    c_ids.wait()
    ids = ids_v[...]
    high = ids // 256
    low = ids - high * 256
    spread = (
        lax.broadcasted_iota(jnp.int32, (REQ, ROWS), 0)
        == lax.broadcasted_iota(jnp.int32, (REQ, ROWS), 1) // TOK
    ).astype(F32).astype(BF)
    wide = mm(high.astype(F32).astype(BF), spread) * 256.0 + mm(low.astype(F32).astype(BF), spread)
    pick = lax.broadcasted_iota(jnp.int32, (TOK, ROWS), 0) == (
        lax.broadcasted_iota(jnp.int32, (TOK, ROWS), 1) % TOK
    )
    id_row = jnp.sum(jnp.where(pick, wide, 0.0), 0, keepdims=True).astype(jnp.int32)
    id_row = id_row - me_m * VR
    selector = (
        (lax.broadcasted_iota(jnp.int32, (VR, ROWS), 0) == id_row).astype(F32).astype(BF)
    )
    c_emb.wait()
    c_ad0 = fetch(adown_hbm.at[0], ad_v.at[pl.ds(0, F)])
    c_ad1 = fetch(adown_hbm.at[1], ad_v.at[pl.ds(FP, F)])
    c_wq0 = fetch(wqkv_hbm.at[0], wq_v.at[:, pl.ds(0, F)])
    c_wq1 = fetch(wqkv_hbm.at[1], wq_v.at[:, pl.ds(FP, F)])
    c_aup = fetch(aup_hbm, aup_v)
    found = mm(emb_v[...], selector)
    found = jnp.concatenate([found, jnp.zeros((pad, ROWS), F32)], 0)
    es_v[me_m] = found.T.astype(BF)

    pl.semaphore_wait(barrier, NS + NM - 2)

    each_mp(lambda p: send(es_v.at[me_m], es_v.at[me_m], 0, "mp", p))

    c_len = fetch(len_hbm, len_s)
    c_kc = fetch(kc_hbm, kc_v)
    c_vc = fetch(vc_hbm, vc_v)
    c_wo = fetch(wout_hbm, wo_v.at[pl.ds(0, F)])
    c_fg = fetch(fgain_hbm, fgain_v)
    c_fup = fetch(fup_hbm, fup_v)
    c_fd = fetch(fdown_hbm, fd_v.at[pl.ds(0, F)])
    c_gate = fetch(gate_hbm, gate_v.at[pl.ds(0, F)])
    c_upm = fetch(upm_hbm, upm_v.at[pl.ds(0, F)])
    c_dn = fetch(down_hbm, dn_v.at[pl.ds(0, F)])
    c_hid.wait()
    c_gain.wait()
    for b in range(REQ):
        h_v[pl.ds(TOK * b, TOK), pl.ds(0, F)] = hid_v[b].astype(F32)
    gains = gain_v[...].astype(F32)
    gains = jnp.concatenate([gains, jnp.zeros((2, pad), F32)], 1)
    state = h_v[...]
    scaled_h = (state * gains[0:1]).astype(BF)
    c_ad0.wait()
    c_ad1.wait()
    c_aup.wait()
    c_wq0.wait()
    c_wq1.wait()
    low_h = mm(scaled_h, ad_v[pl.ds(0, FP), :]).astype(BF)
    low_w = ad_v[pl.ds(FP, FP), :]
    for part in range(3):
        ph_v[part] = mm(scaled_h, wq_v[part, pl.ds(0, FP), :]) + mm(low_h, aup_v[part])
        wq_v[part, pl.ds(FP, FP), :] = (
            wq_v[part, pl.ds(FP, FP), :].astype(F32) + mm(low_w, aup_v[part])
        ).astype(BF)
    squares_h = jnp.sum(state * state, 1, keepdims=True)

    took(es_v.at[pl.ds(0, NM - 1)], rsem.at[0])
    embed = es_v[0].astype(F32)
    for q in range(1, NM):
        embed = embed + es_v[q].astype(F32)
    scaled_e = (embed * gains[1:2]).astype(BF)
    squares = squares_h + jnp.sum(embed * embed, 1, keepdims=True)
    on_lane = lax.broadcasted_iota(jnp.int32, (ROWS, 128), 0) == lax.broadcasted_iota(
        jnp.int32, (ROWS, 128), 1
    )
    squares = jnp.sum(jnp.where(on_lane, squares, 0.0), 0, keepdims=True)
    squares = jnp.broadcast_to(squares, (8, 128))
    lead = squares.astype(BF).astype(F32)
    upper_half = lax.broadcasted_iota(jnp.int32, (8, 128), 0) < 4
    squares = jnp.where(upper_half, lead, squares - lead).astype(BF)

    def project(part, dst, at):
        proj = (ph_v[part] + mm(scaled_e, wq_v[part, pl.ds(FP, FP), :])).astype(BF)
        for j in range(NJ):
            dst[j, :, pl.ds(at, 128)] = proj[:, 128 * j : 128 * j + 128]

    def block_of(ref):
        return lambda i, j: ref.at[j, pl.ds(pl.multiple_of(i * RT, RT), RT)]

    proj = (ph_v[0] + mm(scaled_e, wq_v[0, pl.ds(FP, FP), :])).astype(BF)
    for i in range(NI):
        for j in range(NJ):
            s2_v[i * NJ + j, pl.ds(0, RT), :] = proj[RT * i : RT * i + RT, 128 * j : 128 * j + 128]
            s2_v[i * NJ + j, pl.ds(RT, 8), :] = squares
    scatter(lambda i, j: s2_v.at[i * NJ + j], r2_v.at[me_s], 1)
    c_fup.wait()

    def split(k, carry):
        at = pl.ds(pl.multiple_of(k * 16, 16), 16)
        two = fup_v[at].astype(F32)
        fu_v[0, at, :] = two[:, 0, :].astype(BF)
        fu_v[1, at, :] = two[:, 1, :].astype(BF)
        return carry

    lax.fori_loop(0, 8, split, 0)
    project(1, s2k_v, 0)
    project(2, s2k_v, 128)
    scatter(block_of(s2k_v), r2k_v.at[me_s], 2)
    my_cols = pl.ds(pl.multiple_of(my_j * 128, 128), 128)

    @pl.when(mine)
    def _():
        r2_v[me_s] = s2_v[me_s]
        r2k_v[me_s] = s2k_v[my_j, my_rows, :]
        took(r2_v.at[pl.ds(0, NS - 1)], rsem.at[1])
        total = r2_v[0].astype(F32)
        for s in range(1, NS):
            total = total + r2_v[s].astype(F32)
        sums = jnp.broadcast_to(total[RT : RT + 1] + total[RT + 4 : RT + 5], (RT, 128))
        row_at = lax.broadcasted_iota(jnp.int32, (RT, 128), 0) + my_i * RT
        here = lax.broadcasted_iota(jnp.int32, (RT, 128), 1) == row_at
        sums = jnp.sum(jnp.where(here, sums, 0.0), 1, keepdims=True)
        scale = jnp.broadcast_to(
            1.0 / jnp.sqrt(sums / (2 * MODEL_WIDTH) + EPS), (RT, 128)
        )
        block = gq_v.at[my_rows, my_cols]
        block[...] = (total[:RT] * scale).astype(BF)
        scale_v[...] = scale
        gather(block, 3)

    c_fg.wait()
    c_fd.wait()
    c_gate.wait()
    c_upm.wait()
    for part, w_v in enumerate((gate_v, upm_v)):
        w_v[...] = (w_v[...].astype(F32) + mm(fd_v[...], fu_v[part])).astype(BF)

    @pl.when(mine)
    def _():
        took(r2k_v.at[pl.ds(0, NS - 1)], rsem.at[2])
        total = r2k_v[0].astype(F32)
        for s in range(1, NS):
            total = total + r2k_v[s].astype(F32)
        scale = jnp.concatenate([scale_v[...], scale_v[...]], 1)
        g_v[my_j, my_rows, :] = (total * scale).astype(BF)
        gather(g_v.at[my_j, my_rows], 4)
        took(r2k_v.at[pl.ds(0, OWN - 1), :, pl.ds(0, 128)], rsem.at[3])

    @pl.when(jnp.logical_not(mine))
    def _():
        took(r2k_v.at[pl.ds(0, OWN), :, pl.ds(0, 128)], rsem.at[3])

    lane = lax.broadcasted_iota(jnp.int32, (RT, 128), 1)
    for i in range(NI):
        rows = pl.ds(RT * i, RT)
        for c in range(NJ):
            q = gq_v[rows, pl.ds(128 * c, 128)].astype(F32)
            first, last = (128 * c) // HEAD_DIM, (128 * c + 127) // HEAD_DIM
            for h in range(HEADS):
                if first == last == h:
                    part = q
                elif h in (first, last):
                    part = jnp.where(head_of(lane + 128 * c) == h, q, 0.0)
                else:
                    part = jnp.zeros((RT, 128), F32)
                qm_v[i, pl.ds(RT * h, RT), pl.ds(128 * c, 128)] = part.astype(BF)

    inv_scale = 1.0 / (HEAD_DIM**0.5)
    c_len.wait()
    c_kc.wait()
    c_vc.wait()
    place = me_s * POS + lax.broadcasted_iota(jnp.int32, (HEADS * RT, POS), 1)
    group = (lax.broadcasted_iota(jnp.int32, (HEADS * RT, POS), 0) % RT) // TOK
    per = RT // TOK
    scores = []
    for i in range(NI):
        score = jnp.full((HEADS * RT, POS), DEAD, F32)
        for k in range(per):
            b = per * i + k
            one = mm_nt(qm_v[i], kc_v[b]) * inv_scale
            score = jnp.where((group == k) & (place < len_s[b]), one, score)
        scores.append(score)
    peaks = [jnp.max(score, 1, keepdims=True) for score in scores]
    weights = [
        jnp.where(score > 0.5 * DEAD, jnp.exp(score - peak), 0.0)
        for score, peak in zip(scores, peaks)
    ]
    totals = [jnp.sum(weight, 1, keepdims=True) for weight in weights]
    numers = []
    for i in range(NI):
        spread_w = jnp.concatenate(
            [jnp.where(group == k, weights[i], 0.0).astype(BF) for k in range(per)], 1
        )
        values = vc_v[pl.ds(per * i, per)].reshape(per * POS, CW)
        numers.append(mm(spread_w, values))
    inverses = []
    for i in range(NI):
        live = totals[i] > 0.0
        safe = jnp.where(live, totals[i], 1.0)
        lse = jnp.where(live, peaks[i] + jnp.log(safe), DEAD)
        inverses.append(1.0 / safe)
        stats = jnp.zeros((RT, 128), F32)
        for h in range(HEADS):
            rest = jnp.broadcast_to(lse[RT * h : RT * h + RT], (RT, 128))
            for piece in range(3):
                lead = rest.astype(BF).astype(F32)
                stats = jnp.where(lane == 3 * h + piece, lead, stats)
                rest = rest - lead
        stats = stats.astype(BF)
        for c in range(NJ):
            s4_v[c, pl.ds(RT * i, RT), pl.ds(128, 128)] = stats
    for i in range(NI):
        numer, inverse = numers[i], inverses[i]
        for c in range(NJ):
            first, last = (128 * c) // HEAD_DIM, (128 * c + 127) // HEAD_DIM
            cols = slice(128 * c, 128 * c + 128)
            here = numer[RT * first : RT * first + RT, cols] * inverse[RT * first : RT * first + RT]
            if last != first:
                there = numer[RT * last : RT * last + RT, cols] * inverse[RT * last : RT * last + RT]
                here = jnp.where(head_of(lane + 128 * c) == first, here, there)
            s4_v[c, pl.ds(RT * i, RT), pl.ds(0, 128)] = here.astype(BF)
        for j in range(NJ):
            p = NJ * i + j

            @pl.when(me_s != p)
            def _(i=i, j=j, p=p):
                send(s4_v.at[j, pl.ds(RT * i, RT)], r4_v.at[me_s], 5, "seq", p)


    @pl.when(mine)
    def _():
        took(r2k_v.at[pl.ds(0, OWN - 1)], rsem.at[4])

    @pl.when(jnp.logical_not(mine))
    def _():
        took(r2k_v.at[pl.ds(0, OWN)], rsem.at[4])

    @pl.when(mine)
    def _():
        r4_v[me_s] = s4_v[my_j, my_rows, :]
        lane_head = head_of(lane + 128 * my_j)
        head_a = head_of(128 * my_j)
        head_b = head_of(128 * my_j + 127)
        q = gq_v[my_rows, :].astype(F32)
        k = jnp.concatenate([g_v[c, my_rows, pl.ds(0, 128)] for c in range(NJ)], 1)
        v = g_v[my_j, my_rows, pl.ds(128, 128)]
        col_head = head_of(lax.broadcasted_iota(jnp.int32, (RT, CW), 1))
        r_at = lax.broadcasted_iota(jnp.int32, (RT, RT), 0)
        c_at = lax.broadcasted_iota(jnp.int32, (RT, RT), 1)
        seen = (r_at // TOK == c_at // TOK) & (c_at % TOK <= r_at % TOK)

        def fresh(head):
            score = mm_nt(jnp.where(col_head == head, q, 0.0).astype(BF), k) * inv_scale
            score = jnp.where(seen, score, DEAD)
            peak = jnp.max(score, 1, keepdims=True)
            weight = jnp.where(seen, jnp.exp(score - peak), 0.0)
            total = jnp.sum(weight, 1, keepdims=True)
            return mm(weight.astype(BF), v) / total, peak + jnp.log(total)

        out_a, lse_a = fresh(head_a)
        out_b, lse_b = fresh(head_b)
        new_out = jnp.where(lane_head == head_a, out_a, out_b)
        new_lse = jnp.where(lane_head == head_a, lse_a, lse_b)

        stat_head = lax.broadcasted_iota(jnp.int32, (128, 128), 0) // 3
        expand = (
            (stat_head == head_of(lax.broadcasted_iota(jnp.int32, (128, 128), 1) + 128 * my_j))
            .astype(F32)
            .astype(BF)
        )
        took(r4_v.at[pl.ds(0, NS - 1)], rsem.at[5])
        stats = r4_v[:, :, pl.ds(128, 128)].reshape(NS * RT, 128)
        lse = mm(stats, expand).reshape(NS, RT, 128)
        peak = jnp.maximum(jnp.max(lse, 0), new_lse)
        weight = jnp.exp(lse - peak[None])
        new_weight = jnp.exp(new_lse - peak)
        total = jnp.sum(weight, 0) + new_weight
        numer = jnp.sum(weight * r4_v[:, :, pl.ds(0, 128)].astype(F32), 0) + new_weight * new_out
        block = a_v.at[my_rows, my_cols]
        block[...] = (numer / total).astype(BF)
        gather(block, 6)

    for b in range(REQ):
        for c in range(NJ):
            key_v[b, :, pl.ds(128 * c, 128)] = g_v[c, pl.ds(TOK * b, TOK), pl.ds(0, 128)]
            val_v[b, :, pl.ds(128 * c, 128)] = g_v[c, pl.ds(TOK * b, TOK), pl.ds(128, 128)]
    c_wo.wait()

    @pl.when(mine)
    def _():
        took(r4_v.at[pl.ds(0, OWN - 1), :, pl.ds(0, 128)], rsem.at[6])

    @pl.when(jnp.logical_not(mine))
    def _():
        took(r4_v.at[pl.ds(0, OWN), :, pl.ds(0, 128)], rsem.at[6])

    def sum_mp(part, slot_v, phase, meanwhile=lambda: None):
        slot_v[me_m] = part.astype(BF)
        each_mp(lambda p: send(slot_v.at[me_m], slot_v.at[me_m], phase, "mp", p))
        meanwhile()
        took(slot_v.at[pl.ds(0, NM - 1)], rsem.at[phase])
        total = slot_v[0].astype(F32)
        for q in range(1, NM):
            total = total + slot_v[q].astype(F32)
        return total

    mixed = sum_mp(mm_nt(a_v[...], wo_v[...]), hr_v, 7)
    mid_v[...] = mixed + h_v[...]
    fgain = jnp.concatenate([fgain_v[...].astype(F32), jnp.zeros((1, pad), F32)], 1)

    mid = mid_v[...]
    scaled_m = (mid * fgain).astype(BF)
    squares = jnp.broadcast_to(jnp.sum(mid * mid, 1, keepdims=True), (ROWS, 128))

    def partial(j):
        at = pl.ds(pl.multiple_of(j * 256, 256), 256)
        return jnp.concatenate(
            [mm(scaled_m, gate_v[:, at]), mm(scaled_m, upm_v[:, at]), squares], 1
        )

    sibling = me_s + 1 - 2 * core
    for k in range(4):
        x7_v[0, k] = partial(3 * (1 - core) + k).astype(BF)
    send(x7_v.at[0], x7_v.at[1], 11, "seq", sibling)
    for k in range(4):
        p7_v[k] = partial(3 * core + k)
    took(x7_v.at[1], rsem.at[11])
    for k in range(4):
        s7_v[k] = (p7_v[k] + x7_v[1, k].astype(F32)).astype(BF)

    def sent_here(i, j):
        upper = jnp.where(i >= NI // 2, 1, 0)
        return jnp.where(j < 3, 0, jnp.where(j > 3, 1, upper)) == core

    def block7(i, j):
        return s7_v.at[j - 3 * core, pl.ds(pl.multiple_of(i * RT, RT), RT)]

    def send7(p):
        i, j = lax.div(p, NJ), lax.rem(p, NJ)

        @pl.when((p < OWN) & sent_here(i, j))
        def _():
            send(block7(i, j), r7_v.at[lax.div(me_s, 2)], 8, "seq", p)

    each_seq(send7)
    own_block = mine & sent_here(my_i, my_j)

    @pl.when(mine)
    def _():
        @pl.when(own_block)
        def _():
            r7_v[lax.div(me_s, 2)] = s7_v[my_j - 3 * core, my_rows, :]
            took(r7_v.at[pl.ds(0, NS // 2 - 1)], rsem.at[8])

        @pl.when(jnp.logical_not(own_block))
        def _():
            took(r7_v.at[pl.ds(0, NS // 2)], rsem.at[8])

        total = r7_v[0].astype(F32)
        for s in range(1, NS // 2):
            total = total + r7_v[s].astype(F32)
        scale = 1.0 / jnp.sqrt(total[:, 512:] / MODEL_WIDTH + EPS)
        scale = jnp.concatenate([scale, scale], 1)
        gate = total[:, 0:256] * scale
        up = total[:, 256:512] * scale
        block = a2_v.at[my_rows, pl.ds(pl.multiple_of(my_j * 256, 256), 256)]
        block[...] = (jax.nn.gelu(gate, approximate=True) * up).astype(BF)
        gather(block, 9)
        took(r4_v.at[pl.ds(0, OWN - 1)], rsem.at[9])

    @pl.when(jnp.logical_not(mine))
    def _():
        took(r4_v.at[pl.ds(0, OWN)], rsem.at[9])

    c_dn.wait()
    down = sum_mp(mm_nt(a2_v[...], dn_v[...]), dr_v, 10)
    updated = (down + mid_v[...]).astype(BF)
    for b in range(REQ):
        upd_v[b] = updated[TOK * b : TOK * b + TOK, :F]

    took(es_v.at[pl.ds(0, NM - 1)], ssem.at[0])
    took(hr_v.at[pl.ds(0, NM - 1)], ssem.at[7])
    took(dr_v.at[pl.ds(0, NM - 1)], ssem.at[10])
    took(x7_v.at[1], ssem.at[11])

    @pl.when(own_block)
    def _():
        took(r7_v.at[pl.ds(0, OWN // 2 - 1)], ssem.at[8])

    @pl.when(jnp.logical_not(own_block))
    def _():
        took(r7_v.at[pl.ds(0, OWN // 2)], ssem.at[8])

    @pl.when(mine)
    def _():
        took(r2_v.at[pl.ds(0, OWN - 1)], ssem.at[1])
        took(r2k_v.at[pl.ds(0, OWN - 1)], ssem.at[2])
        took(r2k_v.at[pl.ds(0, NS - 1), :, pl.ds(0, 128)], ssem.at[3])
        took(r2k_v.at[pl.ds(0, NS - 1)], ssem.at[4])
        took(r4_v.at[pl.ds(0, OWN - 1)], ssem.at[5])
        took(r4_v.at[pl.ds(0, NS - 1), :, pl.ds(0, 128)], ssem.at[6])
        took(r4_v.at[pl.ds(0, NS - 1)], ssem.at[9])

    @pl.when(jnp.logical_not(mine))
    def _():
        took(r2_v.at[pl.ds(0, OWN)], ssem.at[1])
        took(r2k_v.at[pl.ds(0, OWN)], ssem.at[2])
        took(r4_v.at[pl.ds(0, OWN)], ssem.at[5])


def hand_on(a, b, c, a_out, b_out, c_out, sem):
    copies = [
        pltpu.make_async_copy(src, dst, sem.at[k])
        for k, (src, dst) in enumerate(((a, a_out), (b, b_out), (c, c_out)))
    ]
    for copy in copies:
        copy.start()
    for copy in copies:
        copy.wait()


def per_device(
    hidden,
    token_index_list,
    embedding,
    attention_gain,
    query_key_value_matrix,
    attention_adapter_down,
    attention_adapter_up,
    cached_key_rows,
    cached_value_rows,
    lengths,
    output_matrix,
    feedforward_gain,
    gate_matrix,
    up_matrix,
    feedforward_adapter_down,
    feedforward_adapter_up,
    down_matrix,
):
    hbm = pl.BlockSpec(memory_space=pl.ANY)
    inner = pl.BlockSpec(memory_space=pltpu.VMEM)
    vm = pltpu.VMEM
    results = pl.pallas_call(
        kernel,
        name="block",
        out_shape=(vm((REQ, TOK, F), BF), vm((REQ, TOK, CW), BF), vm((REQ, TOK, CW), BF)),
        in_specs=[hbm] * 17,
        out_specs=(inner, inner, inner),
        scratch_shapes=[
            vm((TOK, REQ), jnp.int32),
            pltpu.SMEM((REQ,), jnp.int32),
            vm((REQ, TOK, F), BF),
            vm((F, VR), BF),
            vm((2, F), BF),
            vm((3, 2 * FP, CW), BF),
            vm((2 * FP, 128), BF),
            vm((3, 128, CW), BF),
            vm((REQ, POS, CW), BF),
            vm((REQ, POS, CW), BF),
            vm((FP, CW), BF),
            vm((1, F), BF),
            vm((FP, UW), BF),
            vm((FP, UW), BF),
            vm((FP, 128), BF),
            vm((128, 2, UW), BF),
            vm((2, 128, UW), BF),
            vm((FP, UW), BF),
            vm((ROWS, FP), F32),
            vm((3, ROWS, CW), F32),
            vm((NM, ROWS, FP), BF),
            vm((OWN, RT + 8, 128), BF),
            vm((NS, RT + 8, 128), BF),
            vm((NJ, ROWS, 256), BF),
            vm((NS, RT, 256), BF),
            vm((ROWS, CW), BF),
            vm((NJ, ROWS, 256), BF),
            vm((NI, HEADS * RT, CW), BF),
            vm((NJ, ROWS, 256), BF),
            vm((NS, RT, 256), BF),
            vm((ROWS, CW), BF),
            vm((RT, 128), F32),
            vm((NM, ROWS, FP), BF),
            vm((ROWS, FP), F32),
            vm((2, 4, ROWS, 640), BF),
            vm((4, ROWS, 640), F32),
            vm((4, ROWS, 640), BF),
            vm((NS // 2, RT, 640), BF),
            vm((ROWS, UW), BF),
            vm((NM, ROWS, FP), BF),
            pltpu.SemaphoreType.DMA((24,)),
            pltpu.SemaphoreType.DMA((12,)),
            pltpu.SemaphoreType.DMA((12,)),
        ],
        compiler_params=pltpu.CompilerParams(
            collective_id=0, has_side_effects=True, vmem_limit_bytes=56 * 1024 * 1024
        ),
    )(
        token_index_list.T,
        lengths,
        hidden,
        embedding.T,
        attention_gain,
        jnp.transpose(query_key_value_matrix, (0, 2, 1, 3)),
        attention_adapter_down,
        jnp.transpose(attention_adapter_up, (1, 0, 2)),
        cached_key_rows,
        cached_value_rows,
        output_matrix.T,
        feedforward_gain.reshape(1, F),
        gate_matrix,
        up_matrix,
        feedforward_adapter_down,
        feedforward_adapter_up,
        down_matrix.T,
    )
    results = [pltpu.with_memory_space_constraint(r, pltpu.VMEM) for r in results]
    return pl.pallas_call(
        hand_on,
        name="hand_on",
        out_shape=tuple(jax.ShapeDtypeStruct(r.shape, BF) for r in results),
        in_specs=[inner] * 3,
        out_specs=(hbm, hbm, hbm),
        scratch_shapes=[pltpu.SemaphoreType.DMA((3,))],
    )(*results)


def solution(mesh):
    placed = (
        P(None, None, "seq"),
        P(),
        P("mp", "seq"),
        P(None, "seq"),
        P(None, "seq", None, "mp"),
        P(None, "seq", None),
        P(None, None, "mp"),
        P(None, "seq", "mp"),
        P(None, "seq", "mp"),
        P(),
        P("mp", "seq"),
        P("seq"),
        P("seq", "mp"),
        P("seq", "mp"),
        P("seq", None),
        P(None, None, "mp"),
        P("mp", "seq"),
    )
    return jax.shard_map(
        per_device,
        mesh=mesh,
        in_specs=placed,
        out_specs=(P(None, None, "seq"), P(None, None, "mp"), P(None, None, "mp")),
        check_vma=False,
    )
```
